256 devices in a mesh: gx: 16 (over z, y_lo), gy: 16 (over y_hi, x, core).
Axes of the slice: x: 4, y: 4 (y_hi: 2, y_lo: 2; y = y_hi * 2 + y_lo), z: 8, core: 2. Of those that a mesh axis runs over, the one named last changes fastest.
Arguments:
- psi: float32 [64, 128, 4096], P(None, 'gx', 'gy'), may hold values from -500 to 500
- potential: float32 [128, 4096], P('gx', 'gy'), may hold values from -2 to 0
Outputs:
- orbitals: float32 [64, 128, 4096], P(None, 'gx', 'gy')
The draws below stay inside these ranges and needn't reach their ends.
All inputs are finite; a program needn't handle non-finite values.
Results may differ from the reference program's by a relative error of at most 0.0003.
Values sent between devices are 32-bit elements; how exact they have to be, the bound alone decides.
No kernel may reach another device: no remote copies, remote signals or barrier semaphores. Data moves between devices by JAX's collectives and lax.ppermute only.
A program may use at most 64 MiB of HBM per device.

```python
import math
import jax
import jax.numpy as jnp
from jax import lax

M = 64
NZ = 64
NX = 128
NY = 64


def draw_psi(key, part):
    key_base = jax.random.fold_in(key, 11)
    key_scale = jax.random.fold_in(key, 12)
    key_shared = jax.random.fold_in(key, 13)
    key_offset = jax.random.fold_in(key, 14)
    key_mixing = jax.random.fold_in(key, 15)
    x_ramp = (3.0 ** (jnp.arange(NX, dtype=jnp.float32) / max(NX - 1, 1))).reshape(1, NX, 1)
    offset = jax.random.randint(key_offset, (), 0, M)
    rank_level = ((jnp.arange(M, dtype=jnp.int32) + offset) % M).astype(jnp.float32)
    own_weight = jnp.exp(-rank_level / max(M - 1, 1) * math.log(100.0)).reshape(M, 1, 1)
    shared_weight = jax.random.uniform(key_mixing, (M, 1, 1), jnp.float32, 0.5, 1.5)
    shared = jnp.clip(jax.random.normal(key_shared, (1, NX, NY * NZ), jnp.float32), -6.0, 6.0)
    independent = jnp.clip(jax.random.normal(key_base, (M, NX, NY * NZ), jnp.float32), -6.0, 6.0)
    cell_scale = jnp.exp(jax.random.uniform(key_scale, (1, NX, NY * NZ), jnp.float32) * math.log(10.0))
    values = (shared_weight * shared + own_weight * independent) * cell_scale * x_ramp
    return values.astype(jnp.float32)


def block_levels(key, dims, shards, low, high):
    loudness = 1.0
    for dim, parts in shards:
        steps = jax.random.uniform(jax.random.fold_in(jax.random.fold_in(key, 6), dim), (parts,), jnp.float32, low / len(shards), high / len(shards))
        loudness = loudness * jnp.repeat(jnp.exp(steps), dims[dim] // parts).reshape((-1,) + (1,) * (len(dims) - 1 - dim))
    return loudness


def setup_inputs(seed: int = 0) -> dict:
    key_list = jax.random.split(jax.random.key(seed), 3)
    psi = draw_psi(jax.random.fold_in(key_list[2], 71), 0)
    potential = jnp.clip(-2.0 + 2.0 * jax.random.uniform(key_list[1], (NX, NY * NZ), jnp.float32) ** block_levels(key_list[1], (NX, NY * NZ), ((0, 16), (1, 16)), -0.2, 0.2), -2.0, 0.0)
    return dict(psi=psi, potential=potential)


COEFS = (-205.0 / 72.0, 8.0 / 5.0, -1.0 / 5.0, 8.0 / 315.0, -1.0 / 560.0)
CENTER = 6.5
HALF_WIDTH = 5.5

def hamiltonian(orbital, field_pot):
    laplace = 3.0 * COEFS[0] * orbital
    for distance in range(1, 5):
        for axis_num in range(3):
            laplace = laplace + COEFS[distance] * (jnp.roll(orbital, distance, axis_num) + jnp.roll(orbital, -distance, axis_num))
    return -0.5 * laplace + field_pot * orbital

def orthonormal(matrix, ncount):
    gram_matrix = jnp.dot(matrix, matrix.T, precision=lax.Precision.HIGHEST) / ncount
    lower_factor = jnp.linalg.cholesky(gram_matrix)
    return lax.linalg.triangular_solve(lower_factor, matrix, left_side=True, lower=True)

def reference(psi, potential):
    field_pot = potential.reshape(NX, NY, NZ)

    def filter_one(orbital):
        initial = orbital.reshape(NX, NY, NZ)
        level_one = (hamiltonian(initial, field_pot) - CENTER * initial) / HALF_WIDTH
        second = 2.0 * (hamiltonian(level_one, field_pot) - CENTER * level_one) / HALF_WIDTH - initial
        filtered = 2.0 * (hamiltonian(second, field_pot) - CENTER * second) / HALF_WIDTH - level_one
        return filtered.reshape(NX, NY * NZ)
    filtered = lax.map(filter_one, psi)
    matrix = filtered.reshape(M, NX * NY * NZ)
    ncount = float(NX * NY * NZ)
    first_pass = orthonormal(matrix, ncount)
    final_pass = orthonormal(first_pass, ncount)
    return final_pass.reshape(M, NX, NY * NZ)
```

```python
import functools
import math

import jax
import jax.numpy as jnp
from jax import lax
from jax.experimental import pallas as pl
from jax.experimental.pallas import tpu as pltpu
from jax.sharding import PartitionSpec as P

NZ = 64


COEFS = (-205.0 / 72.0, 8.0 / 5.0, -1.0 / 5.0, 8.0 / 315.0, -1.0 / 560.0)
CENTER = 6.5
HALF_WIDTH = 5.5
VMEM = pl.BlockSpec(memory_space=pltpu.VMEM)
NT = (((1,), (1,)), ((), ()))


def padded(array, sides, width):
    for axis, dim in sides:
        size, length = (lax.axis_size(axis), array.shape[dim])
        up = [(i, (i + 1) % size) for i in range(size)]
        down = [(j, i) for i, j in up]
        last = lax.slice_in_dim(array, length - width, length, axis=dim)
        first = lax.slice_in_dim(array, 0, width, axis=dim)
        before = lax.ppermute(last, axis, up)
        after = lax.ppermute(first, axis, down)
        array = jnp.concatenate([before, array, after], axis=dim)
    return array


def along_third(field, depth_index):
    laplace = 3.0 * COEFS[0] * field
    for distance in range(1, 5):
        forward = jnp.where(
            depth_index < NZ - distance,
            jnp.roll(field, -distance, 2),
            jnp.roll(field, NZ - distance, 2),
        )
        behind = jnp.where(
            depth_index >= distance, jnp.roll(field, distance, 2), jnp.roll(field, distance - NZ, 2)
        )
        laplace = laplace + COEFS[distance] * (forward + behind)
    return laplace


def hamiltonian(field, field_pot, depth_index):
    row_count = field.shape[1]
    lane_count = field.shape[2]
    padded_x = padded(field, (("gx", 1),), 4)
    laplace = along_third(field, depth_index)
    padded_y = padded(field, (("gy", 2),), 4 * NZ)
    for distance in range(1, 5):
        laplace = laplace + COEFS[distance] * (
            padded_x[:, 4 + distance : 4 + distance + row_count]
            + padded_x[:, 4 - distance : 4 - distance + row_count]
        )
        ahead_start = (4 + distance) * NZ
        back_start = (4 - distance) * NZ
        laplace = laplace + COEFS[distance] * (
            padded_y[:, :, ahead_start : ahead_start + lane_count]
            + padded_y[:, :, back_start : back_start + lane_count]
        )
    return -0.5 * laplace + field_pot * field


def two_sum(a, b):
    s = a + b
    t = s - a
    return s, (a - (s - t)) + (b - t)


def slices(hi, lo, count, shift, bits):
    top = jnp.max(jnp.abs(hi), axis=1, keepdims=True)
    rest, out = hi, []
    for k in range(count):
        if k == 3 and lo is not None:
            rest = rest + lo
        grain = top * (1.5 * 2.0 ** (shift - bits * k))
        part = (rest + grain) - grain
        rest = rest - part
        out.append(part.astype(jnp.bfloat16))
    return out, rest


def gram_kernel(x_ref, o_ref):
    m, rows, _ = x_ref.shape
    top = jnp.max(jnp.abs(x_ref[:, 0, :]), axis=1, keepdims=True)
    for r in range(1, rows):
        top = jnp.maximum(top, jnp.max(jnp.abs(x_ref[:, r, :]), axis=1, keepdims=True))
    g0 = top * (1.5 * 2.0**17)
    g1 = top * (1.5 * 2.0**11)
    total = None
    for r in range(rows):
        x = x_ref[:, r, :]
        s0 = (x + g0) - g0
        x = x - s0
        s1 = (x + g1) - g1
        x = x - s1
        s2 = x.astype(jnp.bfloat16)
        s3 = (x - s2.astype(jnp.float32)).astype(jnp.bfloat16)
        z = jnp.concatenate([s0.astype(jnp.bfloat16), s1.astype(jnp.bfloat16), s2, s3], axis=0)
        part = lax.dot_general(z, z, NT, preferred_element_type=jnp.float32)
        total = part if total is None else total + part

    def block(a, b):
        return total[a * m : (a + 1) * m, b * m : (b + 1) * m]

    hi, lo = two_sum(block(0, 0), block(0, 1) + block(1, 0))
    small = block(0, 3) + block(3, 0) + block(1, 2) + block(2, 1)
    small = small + (block(1, 3) + block(3, 1) + block(2, 2))
    lo = lo + ((block(1, 1) + (block(0, 2) + block(2, 0))) + small)
    hi, lo = two_sum(hi, lo)
    h = m // 2
    o_ref[:h, :] = jnp.concatenate([hi[:h], hi[h:]], axis=1)
    o_ref[h:, :] = jnp.concatenate([lo[:h], lo[h:]], axis=1)


def pair_add(a, b):
    h = a.shape[0] // 2
    s, e = two_sum(a[:h], b[:h])
    s, e = two_sum(s, e + (a[h:] + b[h:]))
    return jnp.concatenate([s, e], axis=0)


def reduce_pairs(x):
    def swapped(mask):
        return lax.ppermute(x, ("gx", "gy"), [(i, i ^ mask) for i in range(256)])

    for masks in ((1,), (2,), (6,), (16,), (24,), (32,), (64,), (128,)):
        if len(masks) == 1:
            x = pair_add(x, swapped(masks[0]))
        else:
            a, b, c = (swapped(mask) for mask in masks)
            x = pair_add(pair_add(x, a), pair_add(b, c))
    return x


def lower_inverse(g):
    m = g.shape[0]
    lane = lax.broadcasted_iota(jnp.int32, (8, 2 * m), 1)
    sub = lax.broadcasted_iota(jnp.int32, (8, 2 * m), 0)
    tiles = []
    for t in range(m // 8):
        left = jnp.concatenate([g[8 * t : 8 * t + 8, :]] * 2, axis=1)
        unit = jnp.where(lane == sub + (8 * t + m), 1.0, 0.0)
        tiles.append(jnp.where(lane < m, left, unit))
    for j in range(m):
        own, s = divmod(j, 8)
        row = jnp.broadcast_to(tiles[own][s : s + 1, :], (8, 2 * m))
        pivot = jnp.broadcast_to(row[:, j : j + 1], (8, 2 * m))
        row = row / pivot
        for t in range(own, m // 8):
            if t == own and s == 7:
                continue
            factor = jnp.broadcast_to(tiles[t][:, j : j + 1], (8, 2 * m))
            if t == own:
                factor = jnp.where(sub > s, factor, 0.0)
            tiles[t] = tiles[t] - factor * row
    out = []
    for t in range(m // 8):
        diag = jnp.sum(jnp.where(lane == sub + 8 * t, tiles[t], 0.0), axis=1, keepdims=True)
        out.append(tiles[t][:, m:] * (1.0 / jnp.sqrt(diag)))
    return jnp.concatenate(out, axis=0)


def exact_product(a_parts, b_parts):
    n, m = len(a_parts), a_parts[0].shape[0]
    p = lax.dot_general(
        jnp.concatenate(a_parts, axis=0),
        jnp.concatenate(b_parts, axis=0),
        NT,
        preferred_element_type=jnp.float32,
    )
    hi = lo = None
    for level in range(n):
        term = None
        for i in range(level + 1):
            j = level - i
            piece = p[i * m : (i + 1) * m, j * m : (j + 1) * m]
            term = piece if term is None else term + piece
        if hi is None:
            hi, lo = term, jnp.zeros_like(term)
        else:
            hi, e = two_sum(hi, term)
            lo = lo + e
    return two_sum(hi, lo)


def rotate_kernel(ncount, p_ref, x_ref, o_ref):
    m, rows, _ = x_ref.shape
    h = m // 2
    hi, lo = p_ref[:h, :] * (1.0 / ncount), p_ref[h:, :] * (1.0 / ncount)
    hi = jnp.concatenate([hi[:, :m], hi[:, m:]], axis=0)
    lo = jnp.concatenate([lo[:, :m], lo[:, m:]], axis=0)
    inverse1 = lower_inverse(hi)
    w_parts, _ = slices(inverse1, None, 6, 16, 7)
    g_parts, _ = slices(hi, lo, 6, 16, 7)
    t_hi, t_lo = exact_product(w_parts, g_parts)
    t_parts, _ = slices(t_hi, t_lo, 6, 16, 7)
    gram2, _ = exact_product(t_parts, w_parts)
    inverse2 = lower_inverse(gram2)
    both = jnp.dot(inverse2, inverse1, precision=lax.Precision.HIGHEST)
    for r in range(rows):
        o_ref[:, r, :] = jnp.dot(both, x_ref[:, r, :], precision=lax.Precision.HIGHEST)


def orthonormal(block, ncount):
    m = block.shape[0]
    local = pl.pallas_call(
        gram_kernel,
        out_shape=jax.ShapeDtypeStruct((m, 2 * m), jnp.float32),
        in_specs=[VMEM],
        out_specs=VMEM,
        name="gram",
    )(block)
    total = reduce_pairs(local)
    return pl.pallas_call(
        functools.partial(rotate_kernel, ncount),
        out_shape=jax.ShapeDtypeStruct(block.shape, jnp.float32),
        in_specs=[VMEM, VMEM],
        out_specs=VMEM,
        name="rotate",
    )(total, block)


def on_device(psi, potential):
    orbit_count, row_count, lane_count = psi.shape
    field_pot = potential.reshape(1, row_count, lane_count)
    depth_index = lax.broadcasted_iota(jnp.int32, (1, 1, lane_count), 2) % NZ
    level_one = (hamiltonian(psi, field_pot, depth_index) - CENTER * psi) / HALF_WIDTH
    second = (
        2.0 * (hamiltonian(level_one, field_pot, depth_index) - CENTER * level_one) / HALF_WIDTH
        - psi
    )
    filtered = (
        2.0 * (hamiltonian(second, field_pot, depth_index) - CENTER * second) / HALF_WIDTH
        - level_one
    )
    ncount = float(row_count * lane_count * lax.axis_size("gx") * lax.axis_size("gy"))
    return orthonormal(filtered, ncount)


def solution(mesh):
    in_specs = (P(None, "gx", "gy"), P("gx", "gy"))
    out_specs = P(None, "gx", "gy")
    return jax.shard_map(
        on_device, mesh=mesh, in_specs=in_specs, out_specs=out_specs, check_vma=False
    )
```

```python
import functools
import math

import jax
import jax.numpy as jnp
from jax import lax
from jax.experimental import pallas as pl
from jax.experimental.pallas import tpu as pltpu
from jax.sharding import PartitionSpec as P

NZ = 64


COEFS = (-205.0 / 72.0, 8.0 / 5.0, -1.0 / 5.0, 8.0 / 315.0, -1.0 / 560.0)
CENTER = 6.5
HALF_WIDTH = 5.5
VMEM = pl.BlockSpec(memory_space=pltpu.VMEM)
NT = (((1,), (1,)), ((), ()))


def padded(array, sides, width):
    for axis, dim in sides:
        size, length = (lax.axis_size(axis), array.shape[dim])
        up = [(i, (i + 1) % size) for i in range(size)]
        down = [(j, i) for i, j in up]
        last = lax.slice_in_dim(array, length - width, length, axis=dim)
        first = lax.slice_in_dim(array, 0, width, axis=dim)
        before = lax.ppermute(last, axis, up)
        after = lax.ppermute(first, axis, down)
        array = jnp.concatenate([before, array, after], axis=dim)
    return array


def along_third(field, depth_index):
    laplace = 3.0 * COEFS[0] * field
    for distance in range(1, 5):
        forward = jnp.where(
            depth_index < NZ - distance,
            jnp.roll(field, -distance, 2),
            jnp.roll(field, NZ - distance, 2),
        )
        behind = jnp.where(
            depth_index >= distance, jnp.roll(field, distance, 2), jnp.roll(field, distance - NZ, 2)
        )
        laplace = laplace + COEFS[distance] * (forward + behind)
    return laplace


def hamiltonian(field, field_pot, depth_index):
    row_count = field.shape[1]
    lane_count = field.shape[2]
    padded_x = padded(field, (("gx", 1),), 4)
    laplace = along_third(field, depth_index)
    padded_y = padded(field, (("gy", 2),), 4 * NZ)
    for distance in range(1, 5):
        laplace = laplace + COEFS[distance] * (
            padded_x[:, 4 + distance : 4 + distance + row_count]
            + padded_x[:, 4 - distance : 4 - distance + row_count]
        )
        ahead_start = (4 + distance) * NZ
        back_start = (4 - distance) * NZ
        laplace = laplace + COEFS[distance] * (
            padded_y[:, :, ahead_start : ahead_start + lane_count]
            + padded_y[:, :, back_start : back_start + lane_count]
        )
    return -0.5 * laplace + field_pot * field


def two_sum(a, b):
    s = a + b
    t = s - a
    return s, (a - (s - t)) + (b - t)


def slices(hi, lo, count, shift, bits):
    top = jnp.max(jnp.abs(hi), axis=1, keepdims=True)
    rest, out = hi, []
    for k in range(count):
        if k == 3 and lo is not None:
            rest = rest + lo
        grain = top * (1.5 * 2.0 ** (shift - bits * k))
        part = (rest + grain) - grain
        rest = rest - part
        out.append(part.astype(jnp.bfloat16))
    return out, rest


def gram_kernel(x_ref, o_ref):
    m, rows, _ = x_ref.shape
    top = jnp.max(jnp.abs(x_ref[:, 0, :]), axis=1, keepdims=True)
    for r in range(1, rows):
        top = jnp.maximum(top, jnp.max(jnp.abs(x_ref[:, r, :]), axis=1, keepdims=True))
    g0 = top * (1.5 * 2.0**17)
    g1 = top * (1.5 * 2.0**11)
    total = None
    for r in range(rows):
        x = x_ref[:, r, :]
        s0 = (x + g0) - g0
        x = x - s0
        s1 = (x + g1) - g1
        x = x - s1
        s2 = x.astype(jnp.bfloat16)
        s3 = (x - s2.astype(jnp.float32)).astype(jnp.bfloat16)
        z = jnp.concatenate([s0.astype(jnp.bfloat16), s1.astype(jnp.bfloat16), s2, s3], axis=0)
        part = lax.dot_general(z, z, NT, preferred_element_type=jnp.float32)
        total = part if total is None else total + part

    def block(a, b):
        return total[a * m : (a + 1) * m, b * m : (b + 1) * m]

    hi, lo = two_sum(block(0, 0), block(0, 1) + block(1, 0))
    small = block(0, 3) + block(3, 0) + block(1, 2) + block(2, 1)
    small = small + (block(1, 3) + block(3, 1) + block(2, 2))
    lo = lo + ((block(1, 1) + (block(0, 2) + block(2, 0))) + small)
    hi, lo = two_sum(hi, lo)
    h = m // 2
    o_ref[:h, :] = jnp.concatenate([hi[:h], hi[h:]], axis=1)
    o_ref[h:, :] = jnp.concatenate([lo[:h], lo[h:]], axis=1)


def pair_add(a, b):
    h = a.shape[0] // 2
    s, e = two_sum(a[:h], b[:h])
    s, e = two_sum(s, e + (a[h:] + b[h:]))
    return jnp.concatenate([s, e], axis=0)


def reduce_pairs(x):
    def swapped(mask):
        return lax.ppermute(x, ("gx", "gy"), [(i, i ^ mask) for i in range(256)])

    for masks in ((1,), (2,), (6,), (16,), (24,), (32,), (64,), (128,)):
        if len(masks) == 1:
            x = pair_add(x, swapped(masks[0]))
        else:
            a, b, c = (swapped(mask) for mask in masks)
            x = pair_add(pair_add(x, a), pair_add(b, c))
    return x


def lower_inverse(g):
    m = g.shape[0]
    b = 8
    shape = (b, 2 * m)
    lane = lax.broadcasted_iota(jnp.int32, shape, 1)
    sub = lax.broadcasted_iota(jnp.int32, shape, 0)
    is_row = [sub == i for i in range(b)]

    def spread(tile, i):
        return jnp.broadcast_to(tile[i : i + 1, :], shape)

    def column(entries):
        out = None
        for i, value in entries:
            out = jnp.where(is_row[i], value, 0.0 if out is None else out)
        return out

    tiles = []
    for t in range(m // b):
        left = jnp.concatenate([g[b * t : b * t + b, :]] * 2, axis=1)
        unit = jnp.where(lane == sub + (b * t + m), 1.0, 0.0)
        tiles.append(jnp.where(lane < m, left, unit))
    out = []
    for k in range(m // b):
        cols = [
            [jnp.broadcast_to(tiles[t][:, b * k + c : b * k + c + 1], shape) for c in range(b)]
            for t in range(k, m // b)
        ]
        a = [[spread(cols[0][c], i) if i >= c else None for c in range(b)] for i in range(b)]
        low = [[None] * b for _ in range(b)]
        inv = []
        for c in range(b):
            r = 1.0 / a[c][c]
            inv.append(r)
            for i in range(c + 1, b):
                low[i][c] = a[i][c] * r
            for j in range(c + 1, b):
                for i in range(j, b):
                    a[i][j] = a[i][j] - low[i][c] * a[j][c]
        y = tiles[k]
        rows = []
        for c in range(b):
            rows.append(spread(y, c))
            if c + 1 < b:
                y = y - column([(i, low[i][c]) for i in range(c + 1, b)]) * rows[c]
        scaled = [rows[c] * inv[c] for c in range(b)]
        for t in range(k + 1, m // b):
            col = cols[t - k]
            for c in range(b):
                for q in range(c):
                    col[c] = col[c] - col[q] * low[c][q]
                tiles[t] = tiles[t] - col[c] * scaled[c]
        root = 1.0 / jnp.sqrt(column(list(enumerate(a[i][i] for i in range(b)))))
        out.append((y * root)[:, m:])
    return jnp.concatenate(out, axis=0)


def exact_product(a_parts, b_parts):
    n, m = len(a_parts), a_parts[0].shape[0]
    p = lax.dot_general(
        jnp.concatenate(a_parts, axis=0),
        jnp.concatenate(b_parts, axis=0),
        NT,
        preferred_element_type=jnp.float32,
    )
    hi = lo = None
    for level in range(n):
        term = None
        for i in range(level + 1):
            j = level - i
            piece = p[i * m : (i + 1) * m, j * m : (j + 1) * m]
            term = piece if term is None else term + piece
        if hi is None:
            hi, lo = term, jnp.zeros_like(term)
        else:
            hi, e = two_sum(hi, term)
            lo = lo + e
    return two_sum(hi, lo)


def rotate_kernel(ncount, p_ref, x_ref, o_ref):
    m, rows, _ = x_ref.shape
    h = m // 2
    hi, lo = p_ref[:h, :] * (1.0 / ncount), p_ref[h:, :] * (1.0 / ncount)
    hi = jnp.concatenate([hi[:, :m], hi[:, m:]], axis=0)
    lo = jnp.concatenate([lo[:, :m], lo[:, m:]], axis=0)
    inverse1 = lower_inverse(hi)
    w_parts, _ = slices(inverse1, None, 6, 16, 7)
    g_parts, _ = slices(hi, lo, 6, 16, 7)
    t_hi, t_lo = exact_product(w_parts, g_parts)
    t_parts, _ = slices(t_hi, t_lo, 6, 16, 7)
    gram2, _ = exact_product(t_parts, w_parts)
    inverse2 = lower_inverse(gram2)
    both = jnp.dot(inverse2, inverse1, precision=lax.Precision.HIGHEST)
    for r in range(rows):
        o_ref[:, r, :] = jnp.dot(both, x_ref[:, r, :], precision=lax.Precision.HIGHEST)


def orthonormal(block, ncount):
    m = block.shape[0]
    local = pl.pallas_call(
        gram_kernel,
        out_shape=jax.ShapeDtypeStruct((m, 2 * m), jnp.float32),
        in_specs=[VMEM],
        out_specs=VMEM,
        name="gram",
    )(block)
    total = reduce_pairs(local)
    return pl.pallas_call(
        functools.partial(rotate_kernel, ncount),
        out_shape=jax.ShapeDtypeStruct(block.shape, jnp.float32),
        in_specs=[VMEM, VMEM],
        out_specs=VMEM,
        name="rotate",
    )(total, block)


def on_device(psi, potential):
    orbit_count, row_count, lane_count = psi.shape
    field_pot = potential.reshape(1, row_count, lane_count)
    depth_index = lax.broadcasted_iota(jnp.int32, (1, 1, lane_count), 2) % NZ
    level_one = (hamiltonian(psi, field_pot, depth_index) - CENTER * psi) / HALF_WIDTH
    second = (
        2.0 * (hamiltonian(level_one, field_pot, depth_index) - CENTER * level_one) / HALF_WIDTH
        - psi
    )
    filtered = (
        2.0 * (hamiltonian(second, field_pot, depth_index) - CENTER * second) / HALF_WIDTH
        - level_one
    )
    ncount = float(row_count * lane_count * lax.axis_size("gx") * lax.axis_size("gy"))
    return orthonormal(filtered, ncount)


def solution(mesh):
    in_specs = (P(None, "gx", "gy"), P("gx", "gy"))
    out_specs = P(None, "gx", "gy")
    return jax.shard_map(
        on_device, mesh=mesh, in_specs=in_specs, out_specs=out_specs, check_vma=False
    )
```

```python
import functools

import jax
import jax.numpy as jnp
import numpy as np
from jax import lax
from jax.experimental import pallas as pl
from jax.experimental.pallas import tpu as pltpu
from jax.sharding import PartitionSpec as P

NZ = 64
AXES = ("gx", "gy")
COEFS = (-205.0 / 72.0, 8.0 / 5.0, -1.0 / 5.0, 8.0 / 315.0, -1.0 / 560.0)
SCALE = 5040
WEIGHTS = (8064, -1008, 128, -9)
CENTER = 6.5
HALF_WIDTH = 5.5
VMEM = pl.BlockSpec(memory_space=pltpu.VMEM)
NT = (((1,), (1,)), ((), ()))
Y_MASKS = (0, 8, 16, 24)


def stencil_matrix(cells):
    lanes = cells * NZ
    out = np.zeros((3 * lanes, lanes), np.float32)
    for j in range(cells):
        for z in range(NZ):
            for d in range(1, 5):
                for s in (-d, d):
                    out[lanes + j * NZ + (z + s) % NZ, j * NZ + z] += WEIGHTS[d - 1]
                    out[lanes + (j + s) * NZ + z, j * NZ + z] += WEIGHTS[d - 1]
    return jnp.asarray(out, jnp.bfloat16)


def place():
    gx, gy = lax.axis_index("gx"), lax.axis_index("gy")
    return gx // 2, gx % 2, gy // 8, (gy % 8) // 2, gy % 2


def permute(x, target):
    return lax.ppermute(x, AXES, [(i, target(i)) for i in range(256)])


def swap(x, mask):
    return permute(x, lambda i: i ^ mask)


def z_even(i):
    return i ^ 32


def z_odd(i):
    z = i // 32
    return (z + (1 if z % 2 else 7)) % 8 * 32 + i % 32


def y_up(i):
    return i // 8 * 8 + (i + 1) % 8


def y_down(i):
    return i // 8 * 8 + (i + 7) % 8


def split_kernel(x_ref, v_ref, *o_refs):
    _, y_lo, y_hi, _, _ = place()
    part = x_ref.shape[0] // 4
    for k, o_ref in enumerate(o_refs):
        q = (y_lo ^ (k // 2)) * 2 + (y_hi ^ (k % 2))
        for r in range(8):
            o_ref[r] = x_ref[pl.ds(q * part, part), r, :]
        o_ref[8, 0:8, :] = v_ref[...]
        o_ref[8, 8:16, :] = v_ref[...]


def send_faces(even, field, p, f1_ref, f2_ref):
    low, high = field[0:4], field[12:16]
    f1_ref[p] = jnp.where(even, high, low)
    f2_ref[p] = jnp.where(even, low, high)


def join_kernel(*refs):
    parts, (f_ref, v_ref, f1_ref, f2_ref) = refs[:4], refs[4:]
    z, y_lo, _, _, _ = place()
    even = z % 2 == 0
    for k, ref in enumerate(parts):
        start = (y_lo ^ (k // 2)) * 8
        f_ref[k % 2, pl.ds(start, 8)] = ref[0:8]
        v = (ref[8, 0:8, :] - (CENTER + 1.5 * COEFS[0])) * (2.0 / HALF_WIDTH)
        for r in range(8):
            v_ref[k % 2, start + r] = jnp.broadcast_to(v[r : r + 1, :], v.shape)
    for p in range(2):
        send_faces(even, f_ref.at[p], p, f1_ref, f2_ref)


def level_kernel(level, *refs):
    f_ref, l_ref, r_ref, z1_ref, z2_ref, v_ref, m_ref = refs[:7]
    refs = refs[7:]
    if level > 1:
        old_ref, refs = refs[0], refs[1:]
    z, y_lo, _, x, core = place()
    even = z % 2 == 0
    rows, orbs, lanes = f_ref.shape[1:]
    flat = (rows * orbs, lanes)
    left_flip = jnp.where((x == 0) & (core == 0), 1, 0)
    right_flip = jnp.where((x == 3) & (core == 1), 1, 0)
    factor = 2.0 if level > 1 else 1.0
    alpha = -0.5 * factor / (HALF_WIDTH * SCALE)
    for p in range(2):
        near = []
        for ref, q in ((l_ref, p ^ left_flip), (f_ref, p), (r_ref, p ^ right_flip)):
            rest = ref[q].reshape(flat)
            pieces = []
            for _ in range(2):
                pieces.append(rest.astype(jnp.bfloat16))
                rest = rest - pieces[-1].astype(jnp.float32)
            near.append(pieces + [rest.astype(jnp.bfloat16)])
        total = None
        for s in (2, 1, 0):
            lhs = jnp.concatenate([near[b][s] for b in range(3)], axis=1)
            term = jnp.dot(lhs, m_ref[...], preferred_element_type=jnp.float32)
            total = term if total is None else total + term
        below = jnp.where(even, z2_ref[p], z1_ref[p])
        above = jnp.where(even, z1_ref[p], z2_ref[p])
        tall = jnp.concatenate([below, f_ref[p], above], axis=0)
        total = total.reshape(rows, orbs, lanes)
        for d in (4, 3, 2, 1):
            pair = tall[4 + d : 4 + d + rows] + tall[4 - d : 4 - d + rows]
            total = total + float(WEIGHTS[d - 1]) * pair
        v = v_ref[p] if level > 1 else 0.5 * v_ref[p]
        v = jnp.concatenate([v] * (orbs // 8), axis=1)
        out = alpha * total + v * f_ref[p]
        if level > 1:
            out = out - old_ref[p]
        if level < 3:
            refs[0][p] = out
            send_faces(even, out, p, refs[1], refs[2])
        else:
            refs[4][...] = out
            for k in (p, p + 2):
                refs[k][...] = refs[4][pl.ds((y_lo ^ (k // 2)) * 8, 8)]


def two_sum(a, b):
    s = a + b
    t = s - a
    return s, (a - (s - t)) + (b - t)


def slices(hi, lo, count, shift, bits):
    top = jnp.max(jnp.abs(hi), axis=1, keepdims=True)
    rest, out = hi, []
    for k in range(count):
        if k == 3 and lo is not None:
            rest = rest + lo
        grain = top * (1.5 * 2.0 ** (shift - bits * k))
        part = (rest + grain) - grain
        rest = rest - part
        out.append(part.astype(jnp.bfloat16))
    return out, rest


def gram_kernel(*refs):
    parts, (x_ref, o_ref) = refs[:4], refs[4:]
    rows, m, _ = x_ref.shape
    _, y_lo, y_hi, _, _ = place()
    for k, ref in enumerate(parts):
        q = (y_lo ^ (k // 2)) * 2 + (y_hi ^ (k % 2))
        x_ref[:, pl.ds(pl.multiple_of(q * (m // 4), m // 4), m // 4), :] = ref[...]
    top = jnp.max(jnp.max(jnp.abs(x_ref[...]), axis=0), axis=1, keepdims=True)
    g0 = top * (1.5 * 2.0**17)
    g1 = top * (1.5 * 2.0**11)
    total = None
    for r in range(rows):
        x = x_ref[r]
        s0 = (x + g0) - g0
        x = x - s0
        s1 = (x + g1) - g1
        x = x - s1
        s2 = x.astype(jnp.bfloat16)
        s3 = (x - s2.astype(jnp.float32)).astype(jnp.bfloat16)
        z = jnp.concatenate([s0.astype(jnp.bfloat16), s1.astype(jnp.bfloat16), s2, s3], axis=0)
        part = lax.dot_general(z, z, NT, preferred_element_type=jnp.float32)
        total = part if total is None else total + part

    def block(a, b):
        return total[a * m : (a + 1) * m, b * m : (b + 1) * m]

    hi, lo = two_sum(block(0, 0), block(0, 1) + block(1, 0))
    small = block(0, 3) + block(3, 0) + block(1, 2) + block(2, 1)
    small = small + (block(1, 3) + block(3, 1) + block(2, 2))
    lo = lo + ((block(1, 1) + (block(0, 2) + block(2, 0))) + small)
    hi, lo = two_sum(hi, lo)
    h = m // 2
    o_ref[:h, :] = jnp.concatenate([hi[:h], hi[h:]], axis=1)
    o_ref[h:, :] = jnp.concatenate([lo[:h], lo[h:]], axis=1)


def pair_add(a, b):
    h = a.shape[0] // 2
    s, e = two_sum(a[:h], b[:h])
    s, e = two_sum(s, e + (a[h:] + b[h:]))
    return jnp.concatenate([s, e], axis=0)


def reduce_pairs(x):
    def swapped(mask):
        return lax.ppermute(x, AXES, [(i, i ^ mask) for i in range(256)])

    for masks in ((1,), (2,), (6,), (16,), (24,), (32,), (64,), (128,)):
        if len(masks) == 1:
            x = pair_add(x, swapped(masks[0]))
        else:
            a, b, c = (swapped(mask) for mask in masks)
            x = pair_add(pair_add(x, a), pair_add(b, c))
    return x


def lower_inverse(g):
    m = g.shape[0]
    b = 8
    shape = (b, 2 * m)
    lane = lax.broadcasted_iota(jnp.int32, shape, 1)
    sub = lax.broadcasted_iota(jnp.int32, shape, 0)
    is_row = [sub == i for i in range(b)]

    def spread(tile, i):
        return jnp.broadcast_to(tile[i : i + 1, :], shape)

    def column(entries):
        out = None
        for i, value in entries:
            out = jnp.where(is_row[i], value, 0.0 if out is None else out)
        return out

    tiles = []
    for t in range(m // b):
        left = jnp.concatenate([g[b * t : b * t + b, :]] * 2, axis=1)
        unit = jnp.where(lane == sub + (b * t + m), 1.0, 0.0)
        tiles.append(jnp.where(lane < m, left, unit))
    out = []
    for k in range(m // b):
        cols = [
            [jnp.broadcast_to(tiles[t][:, b * k + c : b * k + c + 1], shape) for c in range(b)]
            for t in range(k, m // b)
        ]
        a = [[spread(cols[0][c], i) if i >= c else None for c in range(b)] for i in range(b)]
        low = [[None] * b for _ in range(b)]
        inv = []
        for c in range(b):
            r = 1.0 / a[c][c]
            inv.append(r)
            for i in range(c + 1, b):
                low[i][c] = a[i][c] * r
            for j in range(c + 1, b):
                for i in range(j, b):
                    a[i][j] = a[i][j] - low[i][c] * a[j][c]
        y = tiles[k]
        rows = []
        for c in range(b):
            rows.append(spread(y, c))
            if c + 1 < b:
                y = y - column([(i, low[i][c]) for i in range(c + 1, b)]) * rows[c]
        scaled = [rows[c] * inv[c] for c in range(b)]
        for t in range(k + 1, m // b):
            col = cols[t - k]
            for c in range(b):
                for q in range(c):
                    col[c] = col[c] - col[q] * low[c][q]
                tiles[t] = tiles[t] - col[c] * scaled[c]
        root = 1.0 / jnp.sqrt(column(list(enumerate(a[i][i] for i in range(b)))))
        out.append((y * root)[:, m:])
    return jnp.concatenate(out, axis=0)


def exact_product(a_parts, b_parts):
    n, m = len(a_parts), a_parts[0].shape[0]
    p = lax.dot_general(
        jnp.concatenate(a_parts, axis=0),
        jnp.concatenate(b_parts, axis=0),
        NT,
        preferred_element_type=jnp.float32,
    )
    hi = lo = None
    for level in range(n):
        term = None
        for i in range(level + 1):
            j = level - i
            piece = p[i * m : (i + 1) * m, j * m : (j + 1) * m]
            term = piece if term is None else term + piece
        if hi is None:
            hi, lo = term, jnp.zeros_like(term)
        else:
            hi, e = two_sum(hi, term)
            lo = lo + e
    return two_sum(hi, lo)


def rotate_kernel(ncount, p_ref, x_ref, o_ref):
    rows, m, _ = x_ref.shape
    h = m // 2
    hi, lo = p_ref[:h, :] * (1.0 / ncount), p_ref[h:, :] * (1.0 / ncount)
    hi = jnp.concatenate([hi[:, :m], hi[:, m:]], axis=0)
    lo = jnp.concatenate([lo[:, :m], lo[:, m:]], axis=0)
    inverse1 = lower_inverse(hi)
    w_parts, _ = slices(inverse1, None, 6, 16, 7)
    g_parts, _ = slices(hi, lo, 6, 16, 7)
    t_hi, t_lo = exact_product(w_parts, g_parts)
    t_parts, _ = slices(t_hi, t_lo, 6, 16, 7)
    gram2, _ = exact_product(t_parts, w_parts)
    inverse2 = lower_inverse(gram2)
    both = jnp.dot(inverse2, inverse1, precision=lax.Precision.HIGHEST)
    for r in range(rows):
        o_ref[:, r, :] = jnp.dot(both, x_ref[r], precision=lax.Precision.HIGHEST)


def call(kernel, name, outs, *args, scratch=()):
    single = len(outs) == 1
    shapes = [jax.ShapeDtypeStruct(shape, jnp.float32) for shape in outs]
    return pl.pallas_call(
        kernel,
        out_shape=shapes[0] if single else shapes,
        in_specs=[VMEM] * len(args),
        out_specs=VMEM if single else [VMEM] * len(shapes),
        scratch_shapes=[pltpu.VMEM(shape, jnp.float32) for shape in scratch],
        compiler_params=pltpu.CompilerParams(vmem_limit_bytes=32 << 20),
        name=name,
    )(*args)


def on_device(psi, potential):
    m, rows, lanes = psi.shape
    orbs = m // 4
    part = (rows, orbs, lanes)
    field = (2, 2 * rows, orbs, lanes)
    face = (2, 4, orbs, lanes)
    matrix = stencil_matrix(lanes // NZ)
    parts = call(split_kernel, "split", [(rows + 1, orbs, lanes)] * 4, psi, potential)
    parts = [parts[0]] + [swap(parts[k], Y_MASKS[k]) for k in (1, 2, 3)]
    joined = [field, (2, 2 * rows, 8, lanes), face, face]
    now, v, face1, face2 = call(join_kernel, "join", joined, *parts)
    old = None
    for level in (1, 2, 3):
        left, right = permute(now, y_up), permute(now, y_down)
        face1, face2 = permute(face1, z_even), permute(face2, z_odd)
        args = [now, left, right, face1, face2, v, matrix] + ([] if old is None else [old])
        kernel = functools.partial(level_kernel, level)
        if level < 3:
            outs = call(kernel, f"level{level}", [field, face, face], *args)
            old, (now, face1, face2) = now, outs
        else:
            parts = call(kernel, "level3", [part] * 4, *args, scratch=[field[1:]])
    parts = [parts[0]] + [swap(parts[k], Y_MASKS[k]) for k in (1, 2, 3)]
    block, local = call(gram_kernel, "gram", [(rows, m, lanes), (m, 2 * m)], *parts)
    ncount = float(rows * lanes * lax.axis_size("gx") * lax.axis_size("gy"))
    kernel = functools.partial(rotate_kernel, ncount)
    return call(kernel, "rotate", [psi.shape], reduce_pairs(local), block)


def solution(mesh):
    in_specs = (P(None, "gx", "gy"), P("gx", "gy"))
    out_specs = P(None, "gx", "gy")
    return jax.shard_map(
        on_device, mesh=mesh, in_specs=in_specs, out_specs=out_specs, check_vma=False
    )
```

```python
import functools

import jax
import jax.numpy as jnp
import numpy as np
from jax import lax
from jax.experimental import pallas as pl
from jax.experimental.pallas import tpu as pltpu
from jax.sharding import PartitionSpec as P

NZ = 64
AXES = ("gx", "gy")
COEFS = (-205.0 / 72.0, 8.0 / 5.0, -1.0 / 5.0, 8.0 / 315.0, -1.0 / 560.0)
SCALE = 5040
WEIGHTS = (8064, -1008, 128, -9)
CENTER = 6.5
HALF_WIDTH = 5.5
VMEM = pl.BlockSpec(memory_space=pltpu.VMEM)
NT = (((1,), (1,)), ((), ()))
Y_MASKS = (0, 8, 16, 24)


def stencil_matrix(cells):
    lanes = cells * NZ
    out = np.zeros((3 * lanes, lanes), np.float32)
    for j in range(cells):
        for z in range(NZ):
            for d in range(1, 5):
                for s in (-d, d):
                    out[lanes + j * NZ + (z + s) % NZ, j * NZ + z] += WEIGHTS[d - 1]
                    out[lanes + (j + s) * NZ + z, j * NZ + z] += WEIGHTS[d - 1]
    return jnp.asarray(out, jnp.bfloat16)


def place():
    gx, gy = lax.axis_index("gx"), lax.axis_index("gy")
    return gx // 2, gx % 2, gy // 8, (gy % 8) // 2, gy % 2


def permute(x, target):
    return lax.ppermute(x, AXES, [(i, target(i)) for i in range(256)])


def swap(x, mask):
    return permute(x, lambda i: i ^ mask)


def z_even(i):
    return i ^ 32


def z_odd(i):
    z = i // 32
    return (z + (1 if z % 2 else 7)) % 8 * 32 + i % 32


def y_up(i):
    return i // 8 * 8 + (i + 1) % 8


def y_down(i):
    return i // 8 * 8 + (i + 7) % 8


def split_kernel(x_ref, v_ref, *o_refs):
    _, y_lo, y_hi, _, _ = place()
    part = x_ref.shape[0] // 4
    for k, o_ref in enumerate(o_refs):
        q = (y_lo ^ (k // 2)) * 2 + (y_hi ^ (k % 2))
        for r in range(8):
            o_ref[r] = x_ref[pl.ds(q * part, part), r, :]
        o_ref[8, 0:8, :] = v_ref[...]
        o_ref[8, 8:16, :] = v_ref[...]


def send_faces(even, field, p, f1_ref, f2_ref):
    low, high = field[0:4], field[12:16]
    f1_ref[p] = jnp.where(even, high, low)
    f2_ref[p] = jnp.where(even, low, high)


def join_kernel(*refs):
    parts, (f_ref, v_ref, f1_ref, f2_ref) = refs[:4], refs[4:]
    z, y_lo, _, _, _ = place()
    even = z % 2 == 0
    for k, ref in enumerate(parts):
        start = (y_lo ^ (k // 2)) * 8
        f_ref[k % 2, pl.ds(start, 8)] = ref[0:8]
        v = (ref[8, 0:8, :] - (CENTER + 1.5 * COEFS[0])) * (2.0 / HALF_WIDTH)
        for r in range(8):
            v_ref[k % 2, start + r] = jnp.broadcast_to(v[r : r + 1, :], v.shape)
    for p in range(2):
        send_faces(even, f_ref.at[p], p, f1_ref, f2_ref)


def level_kernel(level, *refs):
    f_ref, l_ref, r_ref, z1_ref, z2_ref, v_ref, m_ref = refs[:7]
    refs = refs[7:]
    if level > 1:
        old_ref, refs = refs[0], refs[1:]
    z, y_lo, _, x, core = place()
    even = z % 2 == 0
    rows, orbs, lanes = f_ref.shape[1:]
    flat = (rows * orbs, lanes)
    left_flip = jnp.where((x == 0) & (core == 0), 1, 0)
    right_flip = jnp.where((x == 3) & (core == 1), 1, 0)
    factor = 2.0 if level > 1 else 1.0
    alpha = -0.5 * factor / (HALF_WIDTH * SCALE)
    for p in range(2):
        near = []
        for ref, q in ((l_ref, p ^ left_flip), (f_ref, p), (r_ref, p ^ right_flip)):
            rest = ref[q].reshape(flat)
            pieces = []
            for _ in range(2):
                pieces.append(rest.astype(jnp.bfloat16))
                rest = rest - pieces[-1].astype(jnp.float32)
            near.append(pieces + [rest.astype(jnp.bfloat16)])
        total = None
        for s in (2, 1, 0):
            lhs = jnp.concatenate([near[b][s] for b in range(3)], axis=1)
            term = jnp.dot(lhs, m_ref[...], preferred_element_type=jnp.float32)
            total = term if total is None else total + term
        below = jnp.where(even, z2_ref[p], z1_ref[p])
        above = jnp.where(even, z1_ref[p], z2_ref[p])
        tall = jnp.concatenate([below, f_ref[p], above], axis=0)
        total = total.reshape(rows, orbs, lanes)
        for d in (4, 3, 2, 1):
            pair = tall[4 + d : 4 + d + rows] + tall[4 - d : 4 - d + rows]
            total = total + float(WEIGHTS[d - 1]) * pair
        v = v_ref[p] if level > 1 else 0.5 * v_ref[p]
        v = jnp.concatenate([v] * (orbs // 8), axis=1)
        out = alpha * total + v * f_ref[p]
        if level > 1:
            out = out - old_ref[p]
        if level < 3:
            refs[0][p] = out
            send_faces(even, out, p, refs[1], refs[2])
        else:
            refs[4][...] = out
            for k in (p, p + 2):
                refs[k][...] = refs[4][pl.ds((y_lo ^ (k // 2)) * 8, 8)]


def two_sum(a, b):
    s = a + b
    t = s - a
    return s, (a - (s - t)) + (b - t)


def slices(hi, lo, count, shift, bits):
    top = jnp.max(jnp.abs(hi), axis=1, keepdims=True)
    rest, out = hi, []
    for k in range(count):
        if k == 3 and lo is not None:
            rest = rest + lo
        grain = top * (1.5 * 2.0 ** (shift - bits * k))
        part = (rest + grain) - grain
        rest = rest - part
        out.append(part.astype(jnp.bfloat16))
    return out, rest


def gram_kernel(*refs):
    parts, (x_ref, o_ref) = refs[:4], refs[4:]
    rows, m, _ = x_ref.shape
    _, y_lo, y_hi, _, _ = place()
    for k, ref in enumerate(parts):
        q = (y_lo ^ (k // 2)) * 2 + (y_hi ^ (k % 2))
        x_ref[:, pl.ds(pl.multiple_of(q * (m // 4), m // 4), m // 4), :] = ref[...]
    top = jnp.max(jnp.max(jnp.abs(x_ref[...]), axis=0), axis=1, keepdims=True)
    g0 = top * (1.5 * 2.0**17)
    g1 = top * (1.5 * 2.0**11)
    total = None
    for r in range(rows):
        x = x_ref[r]
        s0 = (x + g0) - g0
        x = x - s0
        s1 = (x + g1) - g1
        x = x - s1
        s2 = x.astype(jnp.bfloat16)
        s3 = (x - s2.astype(jnp.float32)).astype(jnp.bfloat16)
        z = jnp.concatenate([s0.astype(jnp.bfloat16), s1.astype(jnp.bfloat16), s2, s3], axis=0)
        part = lax.dot_general(z, z, NT, preferred_element_type=jnp.float32)
        total = part if total is None else total + part

    def block(a, b):
        return total[a * m : (a + 1) * m, b * m : (b + 1) * m]

    hi, lo = two_sum(block(0, 0), block(0, 1) + block(1, 0))
    small = block(0, 3) + block(3, 0) + block(1, 2) + block(2, 1)
    small = small + (block(1, 3) + block(3, 1) + block(2, 2))
    lo = lo + ((block(1, 1) + (block(0, 2) + block(2, 0))) + small)
    hi, lo = two_sum(hi, lo)
    h = m // 2
    o_ref[:h, :] = jnp.concatenate([hi[:h], hi[h:]], axis=1)
    o_ref[h:, :] = jnp.concatenate([lo[:h], lo[h:]], axis=1)


def pair_add(a, b):
    h = a.shape[0] // 2
    s, e = two_sum(a[:h], b[:h])
    s, e = two_sum(s, e + (a[h:] + b[h:]))
    return jnp.concatenate([s, e], axis=0)


def reduce_pairs(x):
    def swapped(mask):
        return lax.ppermute(x, AXES, [(i, i ^ mask) for i in range(256)])

    for masks in ((1,), (2, 16, 18), (6, 24, 30), (32, 64, 96), (192,)):
        if len(masks) == 1:
            x = pair_add(x, swapped(masks[0]))
        else:
            a, b, c = (swapped(mask) for mask in masks)
            x = pair_add(pair_add(x, a), pair_add(b, c))
    return x


def lower_inverse(g):
    m = g.shape[0]
    b = 8
    shape = (b, 2 * m)
    lane = lax.broadcasted_iota(jnp.int32, shape, 1)
    sub = lax.broadcasted_iota(jnp.int32, shape, 0)
    is_row = [sub == i for i in range(b)]

    def spread(tile, i):
        return jnp.broadcast_to(tile[i : i + 1, :], shape)

    def column(entries):
        out = None
        for i, value in entries:
            out = jnp.where(is_row[i], value, 0.0 if out is None else out)
        return out

    tiles = []
    for t in range(m // b):
        left = jnp.concatenate([g[b * t : b * t + b, :]] * 2, axis=1)
        unit = jnp.where(lane == sub + (b * t + m), 1.0, 0.0)
        tiles.append(jnp.where(lane < m, left, unit))
    out = []
    for k in range(m // b):
        cols = [
            [jnp.broadcast_to(tiles[t][:, b * k + c : b * k + c + 1], shape) for c in range(b)]
            for t in range(k, m // b)
        ]
        a = [[spread(cols[0][c], i) if i >= c else None for c in range(b)] for i in range(b)]
        low = [[None] * b for _ in range(b)]
        inv = []
        for c in range(b):
            r = 1.0 / a[c][c]
            inv.append(r)
            for i in range(c + 1, b):
                low[i][c] = a[i][c] * r
            for j in range(c + 1, b):
                for i in range(j, b):
                    a[i][j] = a[i][j] - low[i][c] * a[j][c]
        y = tiles[k]
        rows = []
        for c in range(b):
            rows.append(spread(y, c))
            if c + 1 < b:
                y = y - column([(i, low[i][c]) for i in range(c + 1, b)]) * rows[c]
        scaled = [rows[c] * inv[c] for c in range(b)]
        for t in range(k + 1, m // b):
            col = cols[t - k]
            for c in range(b):
                for q in range(c):
                    col[c] = col[c] - col[q] * low[c][q]
                tiles[t] = tiles[t] - col[c] * scaled[c]
        root = 1.0 / jnp.sqrt(column(list(enumerate(a[i][i] for i in range(b)))))
        out.append((y * root)[:, m:])
    return jnp.concatenate(out, axis=0)


def exact_product(a_parts, b_parts):
    n, m = len(a_parts), a_parts[0].shape[0]
    p = lax.dot_general(
        jnp.concatenate(a_parts, axis=0),
        jnp.concatenate(b_parts, axis=0),
        NT,
        preferred_element_type=jnp.float32,
    )
    hi = lo = None
    for level in range(n):
        term = None
        for i in range(level + 1):
            j = level - i
            piece = p[i * m : (i + 1) * m, j * m : (j + 1) * m]
            term = piece if term is None else term + piece
        if hi is None:
            hi, lo = term, jnp.zeros_like(term)
        else:
            hi, e = two_sum(hi, term)
            lo = lo + e
    return two_sum(hi, lo)


def rotate_kernel(ncount, p_ref, x_ref, o_ref):
    rows, m, _ = x_ref.shape
    h = m // 2
    hi, lo = p_ref[:h, :] * (1.0 / ncount), p_ref[h:, :] * (1.0 / ncount)
    hi = jnp.concatenate([hi[:, :m], hi[:, m:]], axis=0)
    lo = jnp.concatenate([lo[:, :m], lo[:, m:]], axis=0)
    inverse1 = lower_inverse(hi)
    w_parts, _ = slices(inverse1, None, 6, 16, 7)
    g_parts, _ = slices(hi, lo, 6, 16, 7)
    t_hi, t_lo = exact_product(w_parts, g_parts)
    t_parts, _ = slices(t_hi, t_lo, 6, 16, 7)
    gram2, _ = exact_product(t_parts, w_parts)
    inverse2 = lower_inverse(gram2)
    both = jnp.dot(inverse2, inverse1, precision=lax.Precision.HIGHEST)
    for r in range(rows):
        o_ref[:, r, :] = jnp.dot(both, x_ref[r], precision=lax.Precision.HIGHEST)


def call(kernel, name, outs, *args, scratch=()):
    single = len(outs) == 1
    shapes = [jax.ShapeDtypeStruct(shape, jnp.float32) for shape in outs]
    return pl.pallas_call(
        kernel,
        out_shape=shapes[0] if single else shapes,
        in_specs=[VMEM] * len(args),
        out_specs=VMEM if single else [VMEM] * len(shapes),
        scratch_shapes=[pltpu.VMEM(shape, jnp.float32) for shape in scratch],
        compiler_params=pltpu.CompilerParams(vmem_limit_bytes=32 << 20),
        name=name,
    )(*args)


def on_device(psi, potential):
    m, rows, lanes = psi.shape
    orbs = m // 4
    part = (rows, orbs, lanes)
    field = (2, 2 * rows, orbs, lanes)
    face = (2, 4, orbs, lanes)
    matrix = stencil_matrix(lanes // NZ)
    parts = call(split_kernel, "split", [(rows + 1, orbs, lanes)] * 4, psi, potential)
    parts = [parts[0]] + [swap(parts[k], Y_MASKS[k]) for k in (1, 2, 3)]
    joined = [field, (2, 2 * rows, 8, lanes), face, face]
    now, v, face1, face2 = call(join_kernel, "join", joined, *parts)
    old = None
    for level in (1, 2, 3):
        left, right = permute(now, y_up), permute(now, y_down)
        face1, face2 = permute(face1, z_even), permute(face2, z_odd)
        args = [now, left, right, face1, face2, v, matrix] + ([] if old is None else [old])
        kernel = functools.partial(level_kernel, level)
        if level < 3:
            outs = call(kernel, f"level{level}", [field, face, face], *args)
            old, (now, face1, face2) = now, outs
        else:
            parts = call(kernel, "level3", [part] * 4, *args, scratch=[field[1:]])
    parts = [parts[0]] + [swap(parts[k], Y_MASKS[k]) for k in (1, 2, 3)]
    block, local = call(gram_kernel, "gram", [(rows, m, lanes), (m, 2 * m)], *parts)
    ncount = float(rows * lanes * lax.axis_size("gx") * lax.axis_size("gy"))
    kernel = functools.partial(rotate_kernel, ncount)
    return call(kernel, "rotate", [psi.shape], reduce_pairs(local), block)


def solution(mesh):
    in_specs = (P(None, "gx", "gy"), P("gx", "gy"))
    out_specs = P(None, "gx", "gy")
    return jax.shard_map(
        on_device, mesh=mesh, in_specs=in_specs, out_specs=out_specs, check_vma=False
    )
```

```python
import functools

import jax
import jax.numpy as jnp
import numpy as np
from jax import lax
from jax.experimental import pallas as pl
from jax.experimental.pallas import tpu as pltpu
from jax.sharding import PartitionSpec as P

NZ = 64
AXES = ("gx", "gy")
COEFS = (-205.0 / 72.0, 8.0 / 5.0, -1.0 / 5.0, 8.0 / 315.0, -1.0 / 560.0)
SCALE = 5040
WEIGHTS = (8064, -1008, 128, -9)
CENTER = 6.5
HALF_WIDTH = 5.5
VMEM = pl.BlockSpec(memory_space=pltpu.VMEM)
NT = (((1,), (1,)), ((), ()))
Y_MASKS = (0, 8, 16, 24)


def stencil_matrix(cells):
    lanes = cells * NZ
    out = np.zeros((3 * lanes, lanes), np.float32)
    for j in range(cells):
        for z in range(NZ):
            for d in range(1, 5):
                for s in (-d, d):
                    out[lanes + j * NZ + (z + s) % NZ, j * NZ + z] += WEIGHTS[d - 1]
                    out[lanes + (j + s) * NZ + z, j * NZ + z] += WEIGHTS[d - 1]
    return jnp.asarray(out, jnp.bfloat16)


def place():
    gx, gy = lax.axis_index("gx"), lax.axis_index("gy")
    return gx // 2, gx % 2, gy // 8, (gy % 8) // 2, gy % 2


def permute(x, target):
    return lax.ppermute(x, AXES, [(i, target(i)) for i in range(256)])


def swap(x, mask):
    return permute(x, lambda i: i ^ mask)


def z_even(i):
    return i ^ 32


def z_odd(i):
    z = i // 32
    return (z + (1 if z % 2 else 7)) % 8 * 32 + i % 32


def y_up(i):
    return i // 8 * 8 + (i + 1) % 8


def y_down(i):
    return i // 8 * 8 + (i + 7) % 8


def split_kernel(x_ref, v_ref, *o_refs):
    _, y_lo, y_hi, _, _ = place()
    part = x_ref.shape[0] // 4
    for k, o_ref in enumerate(o_refs):
        q = (y_lo ^ (k // 2)) * 2 + (y_hi ^ (k % 2))
        for r in range(8):
            o_ref[r] = x_ref[pl.ds(q * part, part), r, :]
        o_ref[8, 0:8, :] = v_ref[...]
        o_ref[8, 8:16, :] = v_ref[...]


def send_faces(even, field, p, f1_ref, f2_ref):
    low, high = field[0:4], field[12:16]
    f1_ref[p] = jnp.where(even, high, low)
    f2_ref[p] = jnp.where(even, low, high)


def join_kernel(*refs):
    parts, (f_ref, v_ref, f1_ref, f2_ref) = refs[:4], refs[4:]
    z, y_lo, _, _, _ = place()
    even = z % 2 == 0
    for k, ref in enumerate(parts):
        start = (y_lo ^ (k // 2)) * 8
        f_ref[k % 2, pl.ds(start, 8)] = ref[0:8]
        v = ref[8, 0:8, :]
        for r in range(8):
            v_ref[k % 2, start + r] = jnp.broadcast_to(v[r : r + 1, :], v.shape)
    for p in range(2):
        send_faces(even, f_ref.at[p], p, f1_ref, f2_ref)


def level_kernel(level, *refs):
    f_ref, l_ref, r_ref, z1_ref, z2_ref, v_ref, m_ref = refs[:7]
    refs = refs[7:]
    if level > 1:
        old_ref, refs = refs[0], refs[1:]
    z, y_lo, _, x, core = place()
    even = z % 2 == 0
    rows, orbs, lanes = f_ref.shape[1:]
    flat = (rows * orbs, lanes)
    left_flip = jnp.where((x == 0) & (core == 0), 1, 0)
    right_flip = jnp.where((x == 3) & (core == 1), 1, 0)
    factor = 2.0 if level > 1 else 1.0
    alpha = -0.5 * factor / (HALF_WIDTH * SCALE)
    for p in range(2):
        near = []
        for ref, q in ((l_ref, p ^ left_flip), (f_ref, p), (r_ref, p ^ right_flip)):
            rest = ref[q].reshape(flat)
            pieces = []
            for _ in range(2):
                pieces.append(rest.astype(jnp.bfloat16))
                rest = rest - pieces[-1].astype(jnp.float32)
            near.append(pieces + [rest.astype(jnp.bfloat16)])
        total = None
        for s in (2, 1, 0):
            lhs = jnp.concatenate([near[b][s] for b in range(3)], axis=1)
            term = jnp.dot(lhs, m_ref[...], preferred_element_type=jnp.float32)
            total = term if total is None else total + term
        below = jnp.where(even, z2_ref[p], z1_ref[p])
        above = jnp.where(even, z1_ref[p], z2_ref[p])
        tall = jnp.concatenate([below, f_ref[p], above], axis=0)
        total = total.reshape(rows, orbs, lanes)
        for d in (4, 3, 2, 1):
            pair = tall[4 + d : 4 + d + rows] + tall[4 - d : 4 - d + rows]
            total = total + float(WEIGHTS[d - 1]) * pair
        v = v_ref[p] if level > 1 else 0.5 * v_ref[p]
        v = jnp.concatenate([v] * (orbs // 8), axis=1)
        out = alpha * total + v * f_ref[p]
        if level > 1:
            out = out - old_ref[p]
        if level < 3:
            refs[0][p] = out
            send_faces(even, out, p, refs[1], refs[2])
        else:
            refs[4][...] = out
            for k in (p, p + 2):
                refs[k][...] = refs[4][pl.ds((y_lo ^ (k // 2)) * 8, 8)]


def two_sum(a, b):
    s = a + b
    t = s - a
    return s, (a - (s - t)) + (b - t)


def slices(hi, lo, count, shift, bits):
    hi = jnp.concatenate([hi, hi], axis=1)
    top = jnp.max(jnp.abs(hi), axis=1, keepdims=True)
    rest, out = hi, []
    for k in range(count):
        if k == 3 and lo is not None:
            rest = rest + jnp.concatenate([lo, lo], axis=1)
        grain = top * (1.5 * 2.0 ** (shift - bits * k))
        part = (rest + grain) - grain
        rest = rest - part
        out.append(part)
    return out


def gram_kernel(*refs):
    parts, (z_ref, o_ref, x_ref) = refs[:4], refs[4:]
    rows, m, _ = x_ref.shape
    _, y_lo, y_hi, _, _ = place()
    for k, ref in enumerate(parts):
        q = (y_lo ^ (k // 2)) * 2 + (y_hi ^ (k % 2))
        x_ref[:, pl.ds(pl.multiple_of(q * (m // 4), m // 4), m // 4), :] = ref[...]
    top = jnp.max(jnp.max(jnp.abs(x_ref[...]), axis=0), axis=1, keepdims=True)
    g0 = top * (1.5 * 2.0**17)
    g1 = top * (1.5 * 2.0**11)
    total = None
    for r in range(rows):
        x = x_ref[r]
        s0 = (x + g0) - g0
        x = x - s0
        s1 = (x + g1) - g1
        x = x - s1
        s2 = x.astype(jnp.bfloat16)
        s3 = (x - s2.astype(jnp.float32)).astype(jnp.bfloat16)
        z = jnp.concatenate([s0.astype(jnp.bfloat16), s1.astype(jnp.bfloat16), s2, s3], axis=0)
        z_ref[r] = z
        part = lax.dot_general(z, z, NT, preferred_element_type=jnp.float32)
        total = part if total is None else total + part

    def block(a, b):
        return total[a * m : (a + 1) * m, b * m : (b + 1) * m]

    hi, lo = two_sum(block(0, 0), block(0, 1) + block(1, 0))
    small = block(0, 3) + block(3, 0) + block(1, 2) + block(2, 1)
    small = small + (block(1, 3) + block(3, 1) + block(2, 2))
    lo = lo + ((block(1, 1) + (block(0, 2) + block(2, 0))) + small)
    hi, lo = two_sum(hi, lo)
    h = m // 2
    o_ref[:h, :] = jnp.concatenate([hi[:h], hi[h:]], axis=1)
    o_ref[h:, :] = jnp.concatenate([lo[:h], lo[h:]], axis=1)


def pair_add(a, b):
    h = a.shape[0] // 2
    s, e = two_sum(a[:h], b[:h])
    s, e = two_sum(s, e + (a[h:] + b[h:]))
    return jnp.concatenate([s, e], axis=0)


def reduce_pairs(x):
    def swapped(mask):
        return lax.ppermute(x, AXES, [(i, i ^ mask) for i in range(256)])

    for masks in ((1,), (2, 16, 18), (6, 24, 30), (32, 64, 96), (192,)):
        if len(masks) == 1:
            x = pair_add(x, swapped(masks[0]))
        else:
            a, b, c = (swapped(mask) for mask in masks)
            x = pair_add(pair_add(x, a), pair_add(b, c))
    return x


def lower_inverse(g):
    m = g.shape[0]
    b = 8
    shape = (b, 2 * m)
    lane = lax.broadcasted_iota(jnp.int32, shape, 1)
    sub = lax.broadcasted_iota(jnp.int32, shape, 0)
    is_row = [sub == i for i in range(b)]

    def spread(tile, i):
        return jnp.broadcast_to(tile[i : i + 1, :], shape)

    def column(entries):
        out = None
        for i, value in entries:
            out = jnp.where(is_row[i], value, 0.0 if out is None else out)
        return out

    tiles = []
    for t in range(m // b):
        left = jnp.concatenate([g[b * t : b * t + b, :]] * 2, axis=1)
        unit = jnp.where(lane == sub + (b * t + m), 1.0, 0.0)
        tiles.append(jnp.where(lane < m, left, unit))
    out = []
    for k in range(m // b):
        cols = [
            [jnp.broadcast_to(tiles[t][:, b * k + c : b * k + c + 1], shape) for c in range(b)]
            for t in range(k, m // b)
        ]
        a = [[spread(cols[0][c], i) if i >= c else None for c in range(b)] for i in range(b)]
        low = [[None] * b for _ in range(b)]
        inv = []
        for c in range(b):
            r = 1.0 / a[c][c]
            inv.append(r)
            for i in range(c + 1, b):
                low[i][c] = a[i][c] * r
            for j in range(c + 1, b):
                for i in range(j, b):
                    a[i][j] = a[i][j] - low[i][c] * a[j][c]
        y = tiles[k]
        rows = []
        for c in range(b):
            rows.append(spread(y, c))
            if c + 1 < b:
                y = y - column([(i, low[i][c]) for i in range(c + 1, b)]) * rows[c]
        scaled = [rows[c] * inv[c] for c in range(b)]
        for t in range(k + 1, m // b):
            col = cols[t - k]
            for c in range(b):
                for q in range(c):
                    col[c] = col[c] - col[q] * low[c][q]
                tiles[t] = tiles[t] - col[c] * scaled[c]
        root = 1.0 / jnp.sqrt(column(list(enumerate(a[i][i] for i in range(b)))))
        out.append((y * root)[:, m:])
    return jnp.concatenate(out, axis=0)


def paired(left, right):
    lane = lax.broadcasted_iota(jnp.int32, left.shape, 1)
    return jnp.where(lane < left.shape[1] // 2, left, right).astype(jnp.bfloat16)


def left_pairs(parts):
    return [paired(parts[i], parts[i + 1]) for i in range(0, len(parts), 2)]


def right_pairs(parts):
    before = [jnp.zeros_like(parts[0])] + parts[:-1]
    return [paired(part, prior) for part, prior in zip(parts, before)]


def exact_product(a_pairs, b_pairs):
    hi = lo = None
    for level in range(len(b_pairs)):
        used = range(0, level + 1, 2)
        term = lax.dot_general(
            jnp.concatenate([a_pairs[i // 2] for i in used], axis=1),
            jnp.concatenate([b_pairs[level - i] for i in used], axis=1),
            NT,
            preferred_element_type=jnp.float32,
        )
        if hi is None:
            hi, lo = term, jnp.zeros_like(term)
        else:
            hi, e = two_sum(hi, term)
            lo = lo + e
    return two_sum(hi, lo)


def rotate_kernel(ncount, p_ref, z_ref, o_ref):
    m, rows, _ = o_ref.shape
    h = m // 2
    hi, lo = p_ref[:h, :] * (1.0 / ncount), p_ref[h:, :] * (1.0 / ncount)
    hi = jnp.concatenate([hi[:, :m], hi[:, m:]], axis=0)
    lo = jnp.concatenate([lo[:, :m], lo[:, m:]], axis=0)
    inverse1 = lower_inverse(hi)
    w_parts = slices(inverse1, None, 6, 16, 7)
    g_parts = slices(hi, lo, 6, 16, 7)
    t_hi, t_lo = exact_product(left_pairs(w_parts), right_pairs(g_parts))
    t_parts = slices(t_hi, t_lo, 6, 16, 7)
    gram2, _ = exact_product(left_pairs(t_parts), right_pairs(w_parts))
    inverse2 = lower_inverse(gram2)
    rest = jnp.dot(inverse2, inverse1, precision=lax.Precision.HIGHEST)
    both = []
    for _ in range(3):
        both.append(rest.astype(jnp.bfloat16))
        rest = rest - both[-1].astype(jnp.float32)
    both = jnp.concatenate([jnp.concatenate([w] * 4, axis=1) for w in both], axis=0)
    for r in range(rows):
        y = jnp.dot(both, z_ref[r], preferred_element_type=jnp.float32)
        o_ref[:, r, :] = y[:m] + (y[m : 2 * m] + y[2 * m :])


def call(kernel, name, outs, *args, scratch=()):
    def typed(spec):
        return spec if isinstance(spec[0], tuple) else (spec, jnp.float32)

    single = len(outs) == 1
    shapes = [jax.ShapeDtypeStruct(*typed(spec)) for spec in outs]
    return pl.pallas_call(
        kernel,
        out_shape=shapes[0] if single else shapes,
        in_specs=[VMEM] * len(args),
        out_specs=VMEM if single else [VMEM] * len(shapes),
        scratch_shapes=[pltpu.VMEM(*typed(spec)) for spec in scratch],
        compiler_params=pltpu.CompilerParams(vmem_limit_bytes=32 << 20),
        name=name,
    )(*args)


def on_device(psi, potential):
    m, rows, lanes = psi.shape
    orbs = m // 4
    part = (rows, orbs, lanes)
    field = (2, 2 * rows, orbs, lanes)
    face = (2, 4, orbs, lanes)
    matrix = stencil_matrix(lanes // NZ)
    own = (potential - (CENTER + 1.5 * COEFS[0])) * (2.0 / HALF_WIDTH)
    parts = call(split_kernel, "split", [(rows + 1, orbs, lanes)] * 4, psi, own)
    parts = [parts[0]] + [swap(parts[k], Y_MASKS[k]) for k in (1, 2, 3)]
    joined = [field, (2, 2 * rows, 8, lanes), face, face]
    now, v, face1, face2 = call(join_kernel, "join", joined, *parts)
    old = None
    for level in (1, 2, 3):
        left, right = permute(now, y_up), permute(now, y_down)
        face1, face2 = permute(face1, z_even), permute(face2, z_odd)
        args = [now, left, right, face1, face2, v, matrix] + ([] if old is None else [old])
        kernel = functools.partial(level_kernel, level)
        if level < 3:
            outs = call(kernel, f"level{level}", [field, face, face], *args)
            old, (now, face1, face2) = now, outs
        else:
            parts = call(kernel, "level3", [part] * 4, *args, scratch=[field[1:]])
    parts = [parts[0]] + [swap(parts[k], Y_MASKS[k]) for k in (1, 2, 3)]
    pieces = ((rows, 4 * m, lanes), jnp.bfloat16)
    whole = [(rows, m, lanes)]
    pieces, local = call(gram_kernel, "gram", [pieces, (m, 2 * m)], *parts, scratch=whole)
    ncount = float(rows * lanes * lax.axis_size("gx") * lax.axis_size("gy"))
    kernel = functools.partial(rotate_kernel, ncount)
    return call(kernel, "rotate", [psi.shape], reduce_pairs(local), pieces)


def solution(mesh):
    in_specs = (P(None, "gx", "gy"), P("gx", "gy"))
    out_specs = P(None, "gx", "gy")
    return jax.shard_map(
        on_device, mesh=mesh, in_specs=in_specs, out_specs=out_specs, check_vma=False
    )
```

```python
import functools

import jax
import jax.numpy as jnp
import numpy as np
from jax import lax
from jax.experimental import pallas as pl
from jax.experimental.pallas import tpu as pltpu
from jax.sharding import PartitionSpec as P

NZ = 64
AXES = ("gx", "gy")
COEFS = (-205.0 / 72.0, 8.0 / 5.0, -1.0 / 5.0, 8.0 / 315.0, -1.0 / 560.0)
SCALE = 5040
WEIGHTS = (8064, -1008, 128, -9)
CENTER = 6.5
HALF_WIDTH = 5.5
VMEM = pl.BlockSpec(memory_space=pltpu.VMEM)
NT = (((1,), (1,)), ((), ()))
Y_MASKS = (0, 8, 16, 24)


def stencil_matrix(cells):
    lanes = cells * NZ
    out = np.zeros((3 * lanes, lanes), np.float32)
    for j in range(cells):
        for z in range(NZ):
            for d in range(1, 5):
                for s in (-d, d):
                    out[lanes + j * NZ + (z + s) % NZ, j * NZ + z] += WEIGHTS[d - 1]
                    out[lanes + (j + s) * NZ + z, j * NZ + z] += WEIGHTS[d - 1]
    return jnp.asarray(out, jnp.bfloat16)


def place():
    gx, gy = lax.axis_index("gx"), lax.axis_index("gy")
    return gx // 2, gx % 2, gy // 8, (gy % 8) // 2, gy % 2


def permute(x, target):
    return lax.ppermute(x, AXES, [(i, target(i)) for i in range(256)])


def swap(x, mask):
    return permute(x, lambda i: i ^ mask)


def z_even(i):
    return i ^ 32


def z_odd(i):
    z = i // 32
    return (z + (1 if z % 2 else 7)) % 8 * 32 + i % 32


def y_up(i):
    return i // 8 * 8 + (i + 1) % 8


def y_down(i):
    return i // 8 * 8 + (i + 7) % 8


def split_kernel(x_ref, v_ref, *o_refs):
    _, y_lo, y_hi, _, _ = place()
    part = x_ref.shape[0] // 4
    for k, o_ref in enumerate(o_refs):
        q = (y_lo ^ (k // 2)) * 2 + (y_hi ^ (k % 2))
        for r in range(8):
            x = x_ref[pl.ds(q * part, part), r, :]
            o_ref[2 * r : 2 * r + 2] = x.reshape(2, 8, x.shape[1])
        o_ref[16] = v_ref[...]


def send_faces(even, field, p, f1_ref, f2_ref):
    low, high = field[0:4], field[12:16]
    f1_ref[p] = jnp.where(even, high, low)
    f2_ref[p] = jnp.where(even, low, high)


def join_kernel(*refs):
    parts, (f_ref, v_ref, f1_ref, f2_ref) = refs[:4], refs[4:]
    z, y_lo, _, _, _ = place()
    even = z % 2 == 0
    for k, ref in enumerate(parts):
        start = (y_lo ^ (k // 2)) * 8
        f_ref[k % 2, pl.ds(start, 8)] = ref[0:16].reshape(8, *f_ref.shape[2:])
        v = ref[16]
        for r in range(8):
            v_ref[k % 2, start + r] = jnp.broadcast_to(v[r : r + 1, :], v.shape)
    for p in range(2):
        send_faces(even, f_ref.at[p], p, f1_ref, f2_ref)


def level_kernel(level, *refs):
    f_ref, l_ref, r_ref, z1_ref, z2_ref, v_ref, m_ref = refs[:7]
    refs = refs[7:]
    if level > 1:
        old_ref, refs = refs[0], refs[1:]
    z, y_lo, _, x, core = place()
    even = z % 2 == 0
    rows, orbs, lanes = f_ref.shape[1:]
    flat = (rows * orbs, lanes)
    left_flip = jnp.where((x == 0) & (core == 0), 1, 0)
    right_flip = jnp.where((x == 3) & (core == 1), 1, 0)
    factor = 2.0 if level > 1 else 1.0
    alpha = -0.5 * factor / (HALF_WIDTH * SCALE)
    for p in range(2):
        near = []
        for ref, q in ((l_ref, p ^ left_flip), (f_ref, p), (r_ref, p ^ right_flip)):
            rest = ref[q].reshape(flat)
            pieces = []
            for _ in range(2):
                pieces.append(rest.astype(jnp.bfloat16))
                rest = rest - pieces[-1].astype(jnp.float32)
            near.append(pieces + [rest.astype(jnp.bfloat16)])
        total = None
        for s in (2, 1, 0):
            lhs = jnp.concatenate([near[b][s] for b in range(3)], axis=1)
            term = jnp.dot(lhs, m_ref[...], preferred_element_type=jnp.float32)
            total = term if total is None else total + term
        below = jnp.where(even, z2_ref[p], z1_ref[p])
        above = jnp.where(even, z1_ref[p], z2_ref[p])
        tall = jnp.concatenate([below, f_ref[p], above], axis=0)
        total = total.reshape(rows, orbs, lanes)
        for d in (4, 3, 2, 1):
            pair = tall[4 + d : 4 + d + rows] + tall[4 - d : 4 - d + rows]
            total = total + float(WEIGHTS[d - 1]) * pair
        v = v_ref[p] if level > 1 else 0.5 * v_ref[p]
        v = jnp.concatenate([v] * (orbs // 8), axis=1)
        out = alpha * total + v * f_ref[p]
        if level > 1:
            out = out - old_ref[p]
        if level < 3:
            refs[0][p] = out
            send_faces(even, out, p, refs[1], refs[2])
        else:
            refs[4][...] = out
            for k in (p, p + 2):
                refs[k][...] = refs[4][pl.ds((y_lo ^ (k // 2)) * 8, 8)]


def two_sum(a, b):
    s = a + b
    t = s - a
    return s, (a - (s - t)) + (b - t)


def slices(hi, lo, count, shift, bits):
    hi = jnp.concatenate([hi, hi], axis=1)
    top = jnp.max(jnp.abs(hi), axis=1, keepdims=True)
    rest, out = hi, []
    for k in range(count):
        if k == 3 and lo is not None:
            rest = rest + jnp.concatenate([lo, lo], axis=1)
        grain = top * (1.5 * 2.0 ** (shift - bits * k))
        part = (rest + grain) - grain
        rest = rest - part
        out.append(part)
    return out


def gram_kernel(*refs):
    parts, (z_ref, o_ref, x_ref) = refs[:4], refs[4:]
    rows, m, _ = x_ref.shape
    _, y_lo, y_hi, _, _ = place()
    for k, ref in enumerate(parts):
        q = (y_lo ^ (k // 2)) * 2 + (y_hi ^ (k % 2))
        x_ref[:, pl.ds(pl.multiple_of(q * (m // 4), m // 4), m // 4), :] = ref[...]
    top = jnp.max(jnp.max(jnp.abs(x_ref[...]), axis=0), axis=1, keepdims=True)
    g0 = top * (1.5 * 2.0**17)
    g1 = top * (1.5 * 2.0**11)
    total = None
    for r in range(rows):
        x = x_ref[r]
        s0 = (x + g0) - g0
        x = x - s0
        s1 = (x + g1) - g1
        x = x - s1
        s2 = x.astype(jnp.bfloat16)
        s3 = (x - s2.astype(jnp.float32)).astype(jnp.bfloat16)
        z = jnp.concatenate([s0.astype(jnp.bfloat16), s1.astype(jnp.bfloat16), s2, s3], axis=0)
        z_ref[r] = z
        part = lax.dot_general(z, z, NT, preferred_element_type=jnp.float32)
        total = part if total is None else total + part

    def block(a, b):
        return total[a * m : (a + 1) * m, b * m : (b + 1) * m]

    hi, lo = two_sum(block(0, 0), block(0, 1) + block(1, 0))
    small = block(0, 3) + block(3, 0) + block(1, 2) + block(2, 1)
    small = small + (block(1, 3) + block(3, 1) + block(2, 2))
    lo = lo + ((block(1, 1) + (block(0, 2) + block(2, 0))) + small)
    hi, lo = two_sum(hi, lo)
    h = m // 2
    o_ref[:h, :] = jnp.concatenate([hi[:h], hi[h:]], axis=1)
    o_ref[h:, :] = jnp.concatenate([lo[:h], lo[h:]], axis=1)


def pair_add(a, b):
    h = a.shape[0] // 2
    s, e = two_sum(a[:h], b[:h])
    s, e = two_sum(s, e + (a[h:] + b[h:]))
    return jnp.concatenate([s, e], axis=0)


def reduce_pairs(x):
    def swapped(mask):
        return lax.ppermute(x, AXES, [(i, i ^ mask) for i in range(256)])

    for masks in ((1,), (2, 32, 34), (16, 64, 80), (6, 24, 30), (192,)):
        if len(masks) == 1:
            x = pair_add(x, swapped(masks[0]))
        else:
            a, b, c = (swapped(mask) for mask in masks)
            x = pair_add(pair_add(x, a), pair_add(b, c))
    return x


def lower_inverse(g):
    m = g.shape[0]
    b = 8
    shape = (b, 2 * m)
    lane = lax.broadcasted_iota(jnp.int32, shape, 1)
    sub = lax.broadcasted_iota(jnp.int32, shape, 0)
    is_row = [sub == i for i in range(b)]

    def spread(tile, i):
        return jnp.broadcast_to(tile[i : i + 1, :], shape)

    def column(entries):
        out = None
        for i, value in entries:
            out = jnp.where(is_row[i], value, 0.0 if out is None else out)
        return out

    tiles = []
    for t in range(m // b):
        left = jnp.concatenate([g[b * t : b * t + b, :]] * 2, axis=1)
        unit = jnp.where(lane == sub + (b * t + m), 1.0, 0.0)
        tiles.append(jnp.where(lane < m, left, unit))
    out = []
    for k in range(m // b):
        cols = [
            [jnp.broadcast_to(tiles[t][:, b * k + c : b * k + c + 1], shape) for c in range(b)]
            for t in range(k, m // b)
        ]
        a = [[spread(cols[0][c], i) if i >= c else None for c in range(b)] for i in range(b)]
        low = [[None] * b for _ in range(b)]
        inv = []
        for c in range(b):
            r = 1.0 / a[c][c]
            inv.append(r)
            for i in range(c + 1, b):
                low[i][c] = a[i][c] * r
            for j in range(c + 1, b):
                for i in range(j, b):
                    a[i][j] = a[i][j] - low[i][c] * a[j][c]
        y = tiles[k]
        rows = []
        for c in range(b):
            rows.append(spread(y, c))
            if c + 1 < b:
                y = y - column([(i, low[i][c]) for i in range(c + 1, b)]) * rows[c]
        scaled = [rows[c] * inv[c] for c in range(b)]
        for t in range(k + 1, m // b):
            col = cols[t - k]
            for c in range(b):
                for q in range(c):
                    col[c] = col[c] - col[q] * low[c][q]
                tiles[t] = tiles[t] - col[c] * scaled[c]
        root = 1.0 / jnp.sqrt(column(list(enumerate(a[i][i] for i in range(b)))))
        out.append((y * root)[:, m:])
    return jnp.concatenate(out, axis=0)


def paired(left, right):
    lane = lax.broadcasted_iota(jnp.int32, left.shape, 1)
    return jnp.where(lane < left.shape[1] // 2, left, right).astype(jnp.bfloat16)


def left_pairs(parts):
    return [paired(parts[i], parts[i + 1]) for i in range(0, len(parts), 2)]


def right_pairs(parts):
    before = [jnp.zeros_like(parts[0])] + parts[:-1]
    return [paired(part, prior) for part, prior in zip(parts, before)]


def exact_product(a_pairs, b_pairs):
    hi = lo = None
    for level in range(len(b_pairs)):
        used = range(0, level + 1, 2)
        term = lax.dot_general(
            jnp.concatenate([a_pairs[i // 2] for i in used], axis=1),
            jnp.concatenate([b_pairs[level - i] for i in used], axis=1),
            NT,
            preferred_element_type=jnp.float32,
        )
        if hi is None:
            hi, lo = term, jnp.zeros_like(term)
        else:
            hi, e = two_sum(hi, term)
            lo = lo + e
    return two_sum(hi, lo)


def rotate_kernel(ncount, p_ref, z_ref, o_ref):
    m, rows, _ = o_ref.shape
    h = m // 2
    hi, lo = p_ref[:h, :] * (1.0 / ncount), p_ref[h:, :] * (1.0 / ncount)
    hi = jnp.concatenate([hi[:, :m], hi[:, m:]], axis=0)
    lo = jnp.concatenate([lo[:, :m], lo[:, m:]], axis=0)
    inverse1 = lower_inverse(hi)
    w_parts = slices(inverse1, None, 6, 16, 7)
    g_parts = slices(hi, lo, 6, 16, 7)
    t_hi, t_lo = exact_product(left_pairs(w_parts), right_pairs(g_parts))
    t_parts = slices(t_hi, t_lo, 6, 16, 7)
    gram2, _ = exact_product(left_pairs(t_parts), right_pairs(w_parts))
    inverse2 = lower_inverse(gram2)
    rest = jnp.dot(inverse2, inverse1, precision=lax.Precision.HIGHEST)
    both = []
    for _ in range(3):
        both.append(rest.astype(jnp.bfloat16))
        rest = rest - both[-1].astype(jnp.float32)
    both = jnp.concatenate([jnp.concatenate([w] * 4, axis=1) for w in both], axis=0)
    for r in range(rows):
        y = jnp.dot(both, z_ref[r], preferred_element_type=jnp.float32)
        o_ref[:, r, :] = y[:m] + (y[m : 2 * m] + y[2 * m :])


def call(kernel, name, outs, *args, scratch=()):
    def typed(spec):
        return spec if isinstance(spec[0], tuple) else (spec, jnp.float32)

    single = len(outs) == 1
    shapes = [jax.ShapeDtypeStruct(*typed(spec)) for spec in outs]
    return pl.pallas_call(
        kernel,
        out_shape=shapes[0] if single else shapes,
        in_specs=[VMEM] * len(args),
        out_specs=VMEM if single else [VMEM] * len(shapes),
        scratch_shapes=[pltpu.VMEM(*typed(spec)) for spec in scratch],
        compiler_params=pltpu.CompilerParams(vmem_limit_bytes=32 << 20),
        name=name,
    )(*args)


def on_device(psi, potential):
    m, rows, lanes = psi.shape
    orbs = m // 4
    part = (rows, orbs, lanes)
    field = (2, 2 * rows, orbs, lanes)
    face = (2, 4, orbs, lanes)
    matrix = stencil_matrix(lanes // NZ)
    own = (potential - (CENTER + 1.5 * COEFS[0])) * (2.0 / HALF_WIDTH)
    parts = call(split_kernel, "split", [(2 * rows + 1, 8, lanes)] * 4, psi, own)
    parts = [parts[0]] + [swap(parts[k], Y_MASKS[k]) for k in (1, 2, 3)]
    joined = [field, (2, 2 * rows, 8, lanes), face, face]
    now, v, face1, face2 = call(join_kernel, "join", joined, *parts)
    old = None
    for level in (1, 2, 3):
        left, right = permute(now, y_up), permute(now, y_down)
        face1, face2 = permute(face1, z_even), permute(face2, z_odd)
        args = [now, left, right, face1, face2, v, matrix] + ([] if old is None else [old])
        kernel = functools.partial(level_kernel, level)
        if level < 3:
            outs = call(kernel, f"level{level}", [field, face, face], *args)
            old, (now, face1, face2) = now, outs
        else:
            parts = call(kernel, "level3", [part] * 4, *args, scratch=[field[1:]])
    parts = [parts[0]] + [swap(parts[k], Y_MASKS[k]) for k in (1, 2, 3)]
    pieces = ((rows, 4 * m, lanes), jnp.bfloat16)
    whole = [(rows, m, lanes)]
    pieces, local = call(gram_kernel, "gram", [pieces, (m, 2 * m)], *parts, scratch=whole)
    ncount = float(rows * lanes * lax.axis_size("gx") * lax.axis_size("gy"))
    kernel = functools.partial(rotate_kernel, ncount)
    return call(kernel, "rotate", [psi.shape], reduce_pairs(local), pieces)


def solution(mesh):
    in_specs = (P(None, "gx", "gy"), P("gx", "gy"))
    out_specs = P(None, "gx", "gy")
    return jax.shard_map(
        on_device, mesh=mesh, in_specs=in_specs, out_specs=out_specs, check_vma=False
    )
```

```python
import functools

import jax
import jax.numpy as jnp
import numpy as np
from jax import lax
from jax.experimental import pallas as pl
from jax.experimental.pallas import tpu as pltpu
from jax.sharding import PartitionSpec as P

NZ = 64
AXES = ("gx", "gy")
COEFS = (-205.0 / 72.0, 8.0 / 5.0, -1.0 / 5.0, 8.0 / 315.0, -1.0 / 560.0)
SCALE = 5040
WEIGHTS = (8064, -1008, 128, -9)
CENTER = 6.5
HALF_WIDTH = 5.5
VMEM = pl.BlockSpec(memory_space=pltpu.VMEM)
NT = (((1,), (1,)), ((), ()))
Y_MASKS = (0, 8, 16, 24)


def stencil_matrix(cells):
    lanes = cells * NZ
    out = np.zeros((3 * lanes, lanes), np.float32)
    for j in range(cells):
        for z in range(NZ):
            for d in range(1, 5):
                for s in (-d, d):
                    out[lanes + j * NZ + (z + s) % NZ, j * NZ + z] += WEIGHTS[d - 1]
                    out[lanes + (j + s) * NZ + z, j * NZ + z] += WEIGHTS[d - 1]
    return jnp.asarray(out, jnp.bfloat16)


def place():
    gx, gy = lax.axis_index("gx"), lax.axis_index("gy")
    return gx // 2, gx % 2, gy // 8, (gy % 8) // 2, gy % 2


def permute(x, target):
    return lax.ppermute(x, AXES, [(i, target(i)) for i in range(256)])


def swap(x, mask):
    return permute(x, lambda i: i ^ mask)


def z_even(i):
    return i ^ 32


def z_odd(i):
    z = i // 32
    return (z + (1 if z % 2 else 7)) % 8 * 32 + i % 32


def y_up(i):
    return i // 8 * 8 + (i + 1) % 8


def y_down(i):
    return i // 8 * 8 + (i + 7) % 8


def split_kernel(x_hbm, v_hbm, *refs):
    o_refs, (x_ref, v_ref, sems) = refs[:4], refs[4:]
    _, y_lo, y_hi, _, _ = place()
    part = x_ref.shape[1]
    copies = [pltpu.make_async_copy(v_hbm, v_ref, sems.at[4])]
    for k in range(4):
        q = (y_lo ^ (k // 2)) * 2 + (y_hi ^ (k % 2))
        source = x_hbm.at[pl.ds(q * part, part)]
        copies.append(pltpu.make_async_copy(source, x_ref.at[k], sems.at[k]))
    for copy in copies:
        copy.start()
    copies[0].wait()
    for k, o_ref in enumerate(o_refs):
        copies[k + 1].wait()
        for r in range(8):
            x = x_ref[k, :, r, :]
            o_ref[2 * r : 2 * r + 2] = x.reshape(2, 8, x.shape[1])
        o_ref[16] = v_ref[...]


def send_faces(even, field, p, f1_ref, f2_ref):
    low, high = field[0:4], field[12:16]
    f1_ref[p] = jnp.where(even, high, low)
    f2_ref[p] = jnp.where(even, low, high)


def join_kernel(*refs):
    parts, (f_ref, v_ref, f1_ref, f2_ref) = refs[:4], refs[4:]
    z, y_lo, _, _, _ = place()
    even = z % 2 == 0
    for k, ref in enumerate(parts):
        start = (y_lo ^ (k // 2)) * 8
        f_ref[k % 2, pl.ds(start, 8)] = ref[0:16].reshape(8, *f_ref.shape[2:])
        v = (ref[16] - (CENTER + 1.5 * COEFS[0])) * (2.0 / HALF_WIDTH)
        for r in range(8):
            v_ref[k % 2, start + r] = jnp.broadcast_to(v[r : r + 1, :], v.shape)
    for p in range(2):
        send_faces(even, f_ref.at[p], p, f1_ref, f2_ref)


def level_kernel(level, *refs):
    f_ref, l_ref, r_ref, z1_ref, z2_ref, v_ref, m_ref = refs[:7]
    refs = refs[7:]
    if level > 1:
        old_ref, refs = refs[0], refs[1:]
    z, y_lo, _, x, core = place()
    even = z % 2 == 0
    rows, orbs, lanes = f_ref.shape[1:]
    flat = (rows * orbs, lanes)
    left_flip = jnp.where((x == 0) & (core == 0), 1, 0)
    right_flip = jnp.where((x == 3) & (core == 1), 1, 0)
    factor = 2.0 if level > 1 else 1.0
    alpha = -0.5 * factor / (HALF_WIDTH * SCALE)
    for p in range(2):
        near = []
        for ref, q in ((l_ref, p ^ left_flip), (f_ref, p), (r_ref, p ^ right_flip)):
            rest = ref[q].reshape(flat)
            pieces = []
            for _ in range(2):
                pieces.append(rest.astype(jnp.bfloat16))
                rest = rest - pieces[-1].astype(jnp.float32)
            near.append(pieces + [rest.astype(jnp.bfloat16)])
        total = None
        for s in (2, 1, 0):
            lhs = jnp.concatenate([near[b][s] for b in range(3)], axis=1)
            term = jnp.dot(lhs, m_ref[...], preferred_element_type=jnp.float32)
            total = term if total is None else total + term
        below = jnp.where(even, z2_ref[p], z1_ref[p])
        above = jnp.where(even, z1_ref[p], z2_ref[p])
        tall = jnp.concatenate([below, f_ref[p], above], axis=0)
        total = total.reshape(rows, orbs, lanes)
        for d in (4, 3, 2, 1):
            pair = tall[4 + d : 4 + d + rows] + tall[4 - d : 4 - d + rows]
            total = total + float(WEIGHTS[d - 1]) * pair
        v = v_ref[p] if level > 1 else 0.5 * v_ref[p]
        v = jnp.concatenate([v] * (orbs // 8), axis=1)
        out = alpha * total + v * f_ref[p]
        if level > 1:
            out = out - old_ref[p]
        if level < 3:
            refs[0][p] = out
            send_faces(even, out, p, refs[1], refs[2])
        else:
            refs[4][...] = out
            for k in (p, p + 2):
                refs[k][...] = refs[4][pl.ds((y_lo ^ (k // 2)) * 8, 8)]


def two_sum(a, b):
    s = a + b
    t = s - a
    return s, (a - (s - t)) + (b - t)


def slices(hi, lo, count, shift, bits):
    hi = jnp.concatenate([hi, hi], axis=1)
    top = jnp.max(jnp.abs(hi), axis=1, keepdims=True)
    rest, out = hi, []
    for k in range(count):
        if k == 3 and lo is not None:
            rest = rest + jnp.concatenate([lo, lo], axis=1)
        grain = top * (1.5 * 2.0 ** (shift - bits * k))
        part = (rest + grain) - grain
        rest = rest - part
        out.append(part)
    return out


def gram_kernel(*refs):
    parts, (z_ref, o_ref, x_ref) = refs[:4], refs[4:]
    rows, m, _ = x_ref.shape
    _, y_lo, y_hi, _, _ = place()
    for k, ref in enumerate(parts):
        q = (y_lo ^ (k // 2)) * 2 + (y_hi ^ (k % 2))
        x_ref[:, pl.ds(pl.multiple_of(q * (m // 4), m // 4), m // 4), :] = ref[...]
    top = jnp.max(jnp.max(jnp.abs(x_ref[...]), axis=0), axis=1, keepdims=True)
    g0 = top * (1.5 * 2.0**17)
    g1 = top * (1.5 * 2.0**11)
    total = None
    for r in range(rows):
        x = x_ref[r]
        s0 = (x + g0) - g0
        x = x - s0
        s1 = (x + g1) - g1
        x = x - s1
        s2 = x.astype(jnp.bfloat16)
        s3 = (x - s2.astype(jnp.float32)).astype(jnp.bfloat16)
        z = jnp.concatenate([s0.astype(jnp.bfloat16), s1.astype(jnp.bfloat16), s2, s3], axis=0)
        z_ref[r] = z
        part = lax.dot_general(z, z, NT, preferred_element_type=jnp.float32)
        total = part if total is None else total + part

    def block(a, b):
        return total[a * m : (a + 1) * m, b * m : (b + 1) * m]

    hi, lo = two_sum(block(0, 0), block(0, 1) + block(1, 0))
    small = block(0, 3) + block(3, 0) + block(1, 2) + block(2, 1)
    small = small + (block(1, 3) + block(3, 1) + block(2, 2))
    lo = lo + ((block(1, 1) + (block(0, 2) + block(2, 0))) + small)
    hi, lo = two_sum(hi, lo)
    h = m // 2
    o_ref[:h, :] = jnp.concatenate([hi[:h], hi[h:]], axis=1)
    o_ref[h:, :] = jnp.concatenate([lo[:h], lo[h:]], axis=1)


def pair_add(a, b):
    h = a.shape[0] // 2
    s, e = two_sum(a[:h], b[:h])
    s, e = two_sum(s, e + (a[h:] + b[h:]))
    return jnp.concatenate([s, e], axis=0)


def reduce_pairs(x):
    def swapped(mask):
        return lax.ppermute(x, AXES, [(i, i ^ mask) for i in range(256)])

    for masks in ((1,), (2, 32, 34), (16, 64, 80), (6, 24, 30), (192,)):
        if len(masks) == 1:
            x = pair_add(x, swapped(masks[0]))
        else:
            a, b, c = (swapped(mask) for mask in masks)
            x = pair_add(pair_add(x, a), pair_add(b, c))
    return x


def lower_inverse(g):
    m = g.shape[0]
    b = 8
    shape = (b, 2 * m)
    lane = lax.broadcasted_iota(jnp.int32, shape, 1)
    sub = lax.broadcasted_iota(jnp.int32, shape, 0)
    is_row = [sub == i for i in range(b)]

    def spread(tile, i):
        return jnp.broadcast_to(tile[i : i + 1, :], shape)

    def column(entries):
        out = None
        for i, value in entries:
            out = jnp.where(is_row[i], value, 0.0 if out is None else out)
        return out

    tiles = []
    for t in range(m // b):
        left = jnp.concatenate([g[b * t : b * t + b, :]] * 2, axis=1)
        unit = jnp.where(lane == sub + (b * t + m), 1.0, 0.0)
        tiles.append(jnp.where(lane < m, left, unit))
    out = []
    for k in range(m // b):
        cols = [
            [jnp.broadcast_to(tiles[t][:, b * k + c : b * k + c + 1], shape) for c in range(b)]
            for t in range(k, m // b)
        ]
        a = [[spread(cols[0][c], i) if i >= c else None for c in range(b)] for i in range(b)]
        low = [[None] * b for _ in range(b)]
        inv = []
        for c in range(b):
            r = 1.0 / a[c][c]
            inv.append(r)
            for i in range(c + 1, b):
                low[i][c] = a[i][c] * r
            for j in range(c + 1, b):
                for i in range(j, b):
                    a[i][j] = a[i][j] - low[i][c] * a[j][c]
        y = tiles[k]
        rows = []
        for c in range(b):
            rows.append(spread(y, c))
            if c + 1 < b:
                y = y - column([(i, low[i][c]) for i in range(c + 1, b)]) * rows[c]
        scaled = [rows[c] * inv[c] for c in range(b)]
        for t in range(k + 1, m // b):
            col = cols[t - k]
            for c in range(b):
                for q in range(c):
                    col[c] = col[c] - col[q] * low[c][q]
                tiles[t] = tiles[t] - col[c] * scaled[c]
        root = 1.0 / jnp.sqrt(column(list(enumerate(a[i][i] for i in range(b)))))
        out.append((y * root)[:, m:])
    return jnp.concatenate(out, axis=0)


def paired(left, right):
    lane = lax.broadcasted_iota(jnp.int32, left.shape, 1)
    return jnp.where(lane < left.shape[1] // 2, left, right).astype(jnp.bfloat16)


def left_pairs(parts):
    return [paired(parts[i], parts[i + 1]) for i in range(0, len(parts), 2)]


def right_pairs(parts):
    before = [jnp.zeros_like(parts[0])] + parts[:-1]
    return [paired(part, prior) for part, prior in zip(parts, before)]


def exact_product(a_pairs, b_pairs):
    hi = lo = None
    for level in range(len(b_pairs)):
        used = range(0, level + 1, 2)
        term = lax.dot_general(
            jnp.concatenate([a_pairs[i // 2] for i in used], axis=1),
            jnp.concatenate([b_pairs[level - i] for i in used], axis=1),
            NT,
            preferred_element_type=jnp.float32,
        )
        if hi is None:
            hi, lo = term, jnp.zeros_like(term)
        else:
            hi, e = two_sum(hi, term)
            lo = lo + e
    return two_sum(hi, lo)


def rotate_kernel(ncount, p_ref, z_ref, o_ref):
    m, rows, _ = o_ref.shape
    h = m // 2
    hi, lo = p_ref[:h, :] * (1.0 / ncount), p_ref[h:, :] * (1.0 / ncount)
    hi = jnp.concatenate([hi[:, :m], hi[:, m:]], axis=0)
    lo = jnp.concatenate([lo[:, :m], lo[:, m:]], axis=0)
    inverse1 = lower_inverse(hi)
    w_parts = slices(inverse1, None, 6, 16, 7)
    g_parts = slices(hi, lo, 6, 16, 7)
    t_hi, t_lo = exact_product(left_pairs(w_parts), right_pairs(g_parts))
    t_parts = slices(t_hi, t_lo, 6, 16, 7)
    gram2, _ = exact_product(left_pairs(t_parts), right_pairs(w_parts))
    inverse2 = lower_inverse(gram2)
    rest = jnp.dot(inverse2, inverse1, precision=lax.Precision.HIGHEST)
    both = []
    for _ in range(3):
        both.append(rest.astype(jnp.bfloat16))
        rest = rest - both[-1].astype(jnp.float32)
    both = jnp.concatenate([jnp.concatenate([w] * 4, axis=1) for w in both], axis=0)
    for r in range(rows):
        y = jnp.dot(both, z_ref[r], preferred_element_type=jnp.float32)
        o_ref[:, r, :] = y[:m] + (y[m : 2 * m] + y[2 * m :])


def call(kernel, name, outs, *args, scratch=()):
    def typed(spec):
        return spec if isinstance(spec[0], tuple) else (spec, jnp.float32)

    single = len(outs) == 1
    shapes = [jax.ShapeDtypeStruct(*typed(spec)) for spec in outs]
    return pl.pallas_call(
        kernel,
        out_shape=shapes[0] if single else shapes,
        in_specs=[VMEM] * len(args),
        out_specs=VMEM if single else [VMEM] * len(shapes),
        scratch_shapes=[pltpu.VMEM(*typed(spec)) for spec in scratch],
        compiler_params=pltpu.CompilerParams(vmem_limit_bytes=32 << 20),
        name=name,
    )(*args)


def on_device(psi, potential):
    m, rows, lanes = psi.shape
    orbs = m // 4
    part = (rows, orbs, lanes)
    field = (2, 2 * rows, orbs, lanes)
    face = (2, 4, orbs, lanes)
    matrix = stencil_matrix(lanes // NZ)
    longer = jax.ShapeDtypeStruct((2 * rows + 1, 8, lanes), jnp.float32)
    parts = pl.pallas_call(
        split_kernel,
        out_shape=[longer] * 4,
        in_specs=[pl.BlockSpec(memory_space=pltpu.HBM)] * 2,
        out_specs=[VMEM] * 4,
        scratch_shapes=[
            pltpu.VMEM((4, orbs, rows, lanes), jnp.float32),
            pltpu.VMEM(potential.shape, jnp.float32),
            pltpu.SemaphoreType.DMA((5,)),
        ],
        compiler_params=pltpu.CompilerParams(vmem_limit_bytes=32 << 20),
        name="split",
    )(
        pltpu.with_memory_space_constraint(psi, pltpu.HBM),
        pltpu.with_memory_space_constraint(potential, pltpu.HBM),
    )
    parts = [parts[0]] + [swap(parts[k], Y_MASKS[k]) for k in (1, 2, 3)]
    joined = [field, (2, 2 * rows, 8, lanes), face, face]
    now, v, face1, face2 = call(join_kernel, "join", joined, *parts)
    old = None
    for level in (1, 2, 3):
        left, right = permute(now, y_up), permute(now, y_down)
        face1, face2 = permute(face1, z_even), permute(face2, z_odd)
        args = [now, left, right, face1, face2, v, matrix] + ([] if old is None else [old])
        kernel = functools.partial(level_kernel, level)
        if level < 3:
            outs = call(kernel, f"level{level}", [field, face, face], *args)
            old, (now, face1, face2) = now, outs
        else:
            parts = call(kernel, "level3", [part] * 4, *args, scratch=[field[1:]])
    parts = [parts[0]] + [swap(parts[k], Y_MASKS[k]) for k in (1, 2, 3)]
    pieces = ((rows, 4 * m, lanes), jnp.bfloat16)
    whole = [(rows, m, lanes)]
    pieces, local = call(gram_kernel, "gram", [pieces, (m, 2 * m)], *parts, scratch=whole)
    ncount = float(rows * lanes * lax.axis_size("gx") * lax.axis_size("gy"))
    kernel = functools.partial(rotate_kernel, ncount)
    return call(kernel, "rotate", [psi.shape], reduce_pairs(local), pieces)


def solution(mesh):
    in_specs = (P(None, "gx", "gy"), P("gx", "gy"))
    out_specs = P(None, "gx", "gy")
    return jax.shard_map(
        on_device, mesh=mesh, in_specs=in_specs, out_specs=out_specs, check_vma=False
    )
```

```python
import functools

import jax
import jax.numpy as jnp
import numpy as np
from jax import lax
from jax.experimental import pallas as pl
from jax.experimental.pallas import tpu as pltpu
from jax.sharding import PartitionSpec as P

NZ = 64
AXES = ("gx", "gy")
COEFS = (-205.0 / 72.0, 8.0 / 5.0, -1.0 / 5.0, 8.0 / 315.0, -1.0 / 560.0)
SCALE = 5040
WEIGHTS = (8064, -1008, 128, -9)
CENTER = 6.5
HALF_WIDTH = 5.5
VMEM = pl.BlockSpec(memory_space=pltpu.VMEM)
NT = (((1,), (1,)), ((), ()))
Y_MASKS = (0, 8, 16, 24)


def stencil_matrix(cells):
    lanes = cells * NZ
    out = np.zeros((3 * lanes, lanes), np.float32)
    for j in range(cells):
        for z in range(NZ):
            for d in range(1, 5):
                for s in (-d, d):
                    out[lanes + j * NZ + (z + s) % NZ, j * NZ + z] += WEIGHTS[d - 1]
                    out[lanes + (j + s) * NZ + z, j * NZ + z] += WEIGHTS[d - 1]
    return jnp.asarray(out, jnp.bfloat16)


def place():
    gx, gy = lax.axis_index("gx"), lax.axis_index("gy")
    return gx // 2, gx % 2, gy // 8, (gy % 8) // 2, gy % 2


def permute(x, target):
    return lax.ppermute(x, AXES, [(i, target(i)) for i in range(256)])


def swap(x, mask):
    return permute(x, lambda i: i ^ mask)


def z_even(i):
    return i ^ 32


def z_odd(i):
    z = i // 32
    return (z + (1 if z % 2 else 7)) % 8 * 32 + i % 32


def y_up(i):
    return i // 8 * 8 + (i + 1) % 8


def y_down(i):
    return i // 8 * 8 + (i + 7) % 8


def split_kernel(x_hbm, v_hbm, *refs):
    o_refs, (x_ref, v_ref, sems) = refs[:4], refs[4:]
    _, y_lo, y_hi, _, _ = place()
    part = x_ref.shape[1]
    copies = [pltpu.make_async_copy(v_hbm, v_ref, sems.at[4])]
    for k in range(4):
        q = (y_lo ^ (k // 2)) * 2 + (y_hi ^ (k % 2))
        source = x_hbm.at[pl.ds(q * part, part)]
        copies.append(pltpu.make_async_copy(source, x_ref.at[k], sems.at[k]))
    for copy in copies:
        copy.start()
    copies[0].wait()
    for k, o_ref in enumerate(o_refs):
        copies[k + 1].wait()
        for r in range(8):
            x = x_ref[k, :, r, :]
            o_ref[2 * r : 2 * r + 2] = x.reshape(2, 8, x.shape[1])
        o_ref[16] = v_ref[...]


def send_faces(even, field, p, f1_ref, f2_ref):
    low, high = field[0:4], field[12:16]
    f1_ref[p] = jnp.where(even, high, low)
    f2_ref[p] = jnp.where(even, low, high)


def join_kernel(*refs):
    parts, (f_ref, v_ref, f1_ref, f2_ref) = refs[:4], refs[4:]
    z, y_lo, _, _, _ = place()
    even = z % 2 == 0
    for k, ref in enumerate(parts):
        start = (y_lo ^ (k // 2)) * 8
        f_ref[k % 2, pl.ds(start, 8)] = ref[0:16].reshape(8, *f_ref.shape[2:])
        v = (ref[16] - (CENTER + 1.5 * COEFS[0])) * (2.0 / HALF_WIDTH)
        for r in range(8):
            v_ref[k % 2, start + r] = jnp.broadcast_to(v[r : r + 1, :], v.shape)
    for p in range(2):
        send_faces(even, f_ref.at[p], p, f1_ref, f2_ref)


def level_kernel(level, patches, *refs):
    f_ref, l_ref, r_ref, z1_ref, z2_ref, v_ref, m_ref = refs[:7]
    refs = refs[7:]
    if level > 1:
        old_ref, refs = refs[0], refs[1:]
    z, y_lo, _, x, core = place()
    even = z % 2 == 0
    rows, orbs, lanes = f_ref.shape[1:]
    flat = (rows * orbs, lanes)
    left_flip = jnp.where((x == 0) & (core == 0), 1, 0)
    right_flip = jnp.where((x == 3) & (core == 1), 1, 0)
    factor = 2.0 if level > 1 else 1.0
    alpha = -0.5 * factor / (HALF_WIDTH * SCALE)
    for p in patches:
        near = []
        for ref, q in ((l_ref, p ^ left_flip), (f_ref, p), (r_ref, p ^ right_flip)):
            rest = ref[q].reshape(flat)
            pieces = []
            for _ in range(2):
                pieces.append(rest.astype(jnp.bfloat16))
                rest = rest - pieces[-1].astype(jnp.float32)
            near.append(pieces + [rest.astype(jnp.bfloat16)])
        total = None
        for s in (2, 1, 0):
            lhs = jnp.concatenate([near[b][s] for b in range(3)], axis=1)
            term = jnp.dot(lhs, m_ref[...], preferred_element_type=jnp.float32)
            total = term if total is None else total + term
        below = jnp.where(even, z2_ref[p], z1_ref[p])
        above = jnp.where(even, z1_ref[p], z2_ref[p])
        tall = jnp.concatenate([below, f_ref[p], above], axis=0)
        total = total.reshape(rows, orbs, lanes)
        for d in (4, 3, 2, 1):
            pair = tall[4 + d : 4 + d + rows] + tall[4 - d : 4 - d + rows]
            total = total + float(WEIGHTS[d - 1]) * pair
        v = v_ref[p] if level > 1 else 0.5 * v_ref[p]
        v = jnp.concatenate([v] * (orbs // 8), axis=1)
        out = alpha * total + v * f_ref[p]
        if level > 1:
            out = out - old_ref[p]
        if level < 3:
            refs[0][p] = out
            send_faces(even, out, p, refs[1], refs[2])
        else:
            refs[2][...] = out
            for k in range(2):
                refs[k][...] = refs[2][pl.ds((y_lo ^ k) * 8, 8)]


def two_sum(a, b):
    s = a + b
    t = s - a
    return s, (a - (s - t)) + (b - t)


def slices(hi, lo, count, shift, bits):
    hi = jnp.concatenate([hi, hi], axis=1)
    top = jnp.max(jnp.abs(hi), axis=1, keepdims=True)
    rest, out = hi, []
    for k in range(count):
        if k == 3 and lo is not None:
            rest = rest + jnp.concatenate([lo, lo], axis=1)
        grain = top * (1.5 * 2.0 ** (shift - bits * k))
        part = (rest + grain) - grain
        rest = rest - part
        out.append(part)
    return out


def gram_kernel(*refs):
    parts, (z_ref, o_ref, x_ref) = refs[:4], refs[4:]
    rows, m, _ = x_ref.shape
    _, y_lo, y_hi, _, _ = place()
    for k, ref in enumerate(parts):
        q = (y_lo ^ (k // 2)) * 2 + (y_hi ^ (k % 2))
        x_ref[:, pl.ds(pl.multiple_of(q * (m // 4), m // 4), m // 4), :] = ref[...]
    top = jnp.max(jnp.max(jnp.abs(x_ref[...]), axis=0), axis=1, keepdims=True)
    g0 = top * (1.5 * 2.0**17)
    g1 = top * (1.5 * 2.0**11)
    total = None
    for r in range(rows):
        x = x_ref[r]
        s0 = (x + g0) - g0
        x = x - s0
        s1 = (x + g1) - g1
        x = x - s1
        s2 = x.astype(jnp.bfloat16)
        s3 = (x - s2.astype(jnp.float32)).astype(jnp.bfloat16)
        z = jnp.concatenate([s0.astype(jnp.bfloat16), s1.astype(jnp.bfloat16), s2, s3], axis=0)
        z_ref[r] = z
        part = lax.dot_general(z, z, NT, preferred_element_type=jnp.float32)
        total = part if total is None else total + part

    def block(a, b):
        return total[a * m : (a + 1) * m, b * m : (b + 1) * m]

    hi, lo = two_sum(block(0, 0), block(0, 1) + block(1, 0))
    small = block(0, 3) + block(3, 0) + block(1, 2) + block(2, 1)
    small = small + (block(1, 3) + block(3, 1) + block(2, 2))
    lo = lo + ((block(1, 1) + (block(0, 2) + block(2, 0))) + small)
    hi, lo = two_sum(hi, lo)
    h = m // 2
    o_ref[:h, :] = jnp.concatenate([hi[:h], hi[h:]], axis=1)
    o_ref[h:, :] = jnp.concatenate([lo[:h], lo[h:]], axis=1)


def pair_add(a, b):
    h = a.shape[0] // 2
    s, e = two_sum(a[:h], b[:h])
    s, e = two_sum(s, e + (a[h:] + b[h:]))
    return jnp.concatenate([s, e], axis=0)


def reduce_pairs(x):
    def swapped(mask):
        return lax.ppermute(x, AXES, [(i, i ^ mask) for i in range(256)])

    for masks in ((1,), (2, 32, 34), (16, 64, 80), (6, 24, 30), (192,)):
        if len(masks) == 1:
            x = pair_add(x, swapped(masks[0]))
        else:
            a, b, c = (swapped(mask) for mask in masks)
            x = pair_add(pair_add(x, a), pair_add(b, c))
    return x


def lower_inverse(g):
    m = g.shape[0]
    b = 8
    shape = (b, 2 * m)
    lane = lax.broadcasted_iota(jnp.int32, shape, 1)
    sub = lax.broadcasted_iota(jnp.int32, shape, 0)
    is_row = [sub == i for i in range(b)]

    def spread(tile, i):
        return jnp.broadcast_to(tile[i : i + 1, :], shape)

    def column(entries):
        out = None
        for i, value in entries:
            out = jnp.where(is_row[i], value, 0.0 if out is None else out)
        return out

    tiles = []
    for t in range(m // b):
        left = jnp.concatenate([g[b * t : b * t + b, :]] * 2, axis=1)
        unit = jnp.where(lane == sub + (b * t + m), 1.0, 0.0)
        tiles.append(jnp.where(lane < m, left, unit))
    out = []
    for k in range(m // b):
        cols = [
            [jnp.broadcast_to(tiles[t][:, b * k + c : b * k + c + 1], shape) for c in range(b)]
            for t in range(k, m // b)
        ]
        a = [[spread(cols[0][c], i) if i >= c else None for c in range(b)] for i in range(b)]
        low = [[None] * b for _ in range(b)]
        inv = []
        for c in range(b):
            r = 1.0 / a[c][c]
            inv.append(r)
            for i in range(c + 1, b):
                low[i][c] = a[i][c] * r
            for j in range(c + 1, b):
                for i in range(j, b):
                    a[i][j] = a[i][j] - low[i][c] * a[j][c]
        y = tiles[k]
        rows = []
        for c in range(b):
            rows.append(spread(y, c))
            if c + 1 < b:
                y = y - column([(i, low[i][c]) for i in range(c + 1, b)]) * rows[c]
        scaled = [rows[c] * inv[c] for c in range(b)]
        for t in range(k + 1, m // b):
            col = cols[t - k]
            for c in range(b):
                for q in range(c):
                    col[c] = col[c] - col[q] * low[c][q]
                tiles[t] = tiles[t] - col[c] * scaled[c]
        root = 1.0 / jnp.sqrt(column(list(enumerate(a[i][i] for i in range(b)))))
        out.append((y * root)[:, m:])
    return jnp.concatenate(out, axis=0)


def paired(left, right):
    lane = lax.broadcasted_iota(jnp.int32, left.shape, 1)
    return jnp.where(lane < left.shape[1] // 2, left, right).astype(jnp.bfloat16)


def left_pairs(parts):
    return [paired(parts[i], parts[i + 1]) for i in range(0, len(parts), 2)]


def right_pairs(parts):
    before = [jnp.zeros_like(parts[0])] + parts[:-1]
    return [paired(part, prior) for part, prior in zip(parts, before)]


def exact_product(a_pairs, b_pairs):
    hi = lo = None
    for level in range(len(b_pairs)):
        used = range(0, level + 1, 2)
        term = lax.dot_general(
            jnp.concatenate([a_pairs[i // 2] for i in used], axis=1),
            jnp.concatenate([b_pairs[level - i] for i in used], axis=1),
            NT,
            preferred_element_type=jnp.float32,
        )
        if hi is None:
            hi, lo = term, jnp.zeros_like(term)
        else:
            hi, e = two_sum(hi, term)
            lo = lo + e
    return two_sum(hi, lo)


def rotate_kernel(ncount, p_ref, z_ref, o_ref):
    m, rows, _ = o_ref.shape
    h = m // 2
    hi, lo = p_ref[:h, :] * (1.0 / ncount), p_ref[h:, :] * (1.0 / ncount)
    hi = jnp.concatenate([hi[:, :m], hi[:, m:]], axis=0)
    lo = jnp.concatenate([lo[:, :m], lo[:, m:]], axis=0)
    inverse1 = lower_inverse(hi)
    w_parts = slices(inverse1, None, 6, 16, 7)
    g_parts = slices(hi, lo, 6, 16, 7)
    t_hi, t_lo = exact_product(left_pairs(w_parts), right_pairs(g_parts))
    t_parts = slices(t_hi, t_lo, 6, 16, 7)
    gram2, _ = exact_product(left_pairs(t_parts), right_pairs(w_parts))
    inverse2 = lower_inverse(gram2)
    rest = jnp.dot(inverse2, inverse1, precision=lax.Precision.HIGHEST)
    both = []
    for _ in range(3):
        both.append(rest.astype(jnp.bfloat16))
        rest = rest - both[-1].astype(jnp.float32)
    both = jnp.concatenate([jnp.concatenate([w] * 4, axis=1) for w in both], axis=0)
    for r in range(rows):
        y = jnp.dot(both, z_ref[r], preferred_element_type=jnp.float32)
        o_ref[:, r, :] = y[:m] + (y[m : 2 * m] + y[2 * m :])


def call(kernel, name, outs, *args, scratch=()):
    def typed(spec):
        return spec if isinstance(spec[0], tuple) else (spec, jnp.float32)

    single = len(outs) == 1
    shapes = [jax.ShapeDtypeStruct(*typed(spec)) for spec in outs]
    return pl.pallas_call(
        kernel,
        out_shape=shapes[0] if single else shapes,
        in_specs=[VMEM] * len(args),
        out_specs=VMEM if single else [VMEM] * len(shapes),
        scratch_shapes=[pltpu.VMEM(*typed(spec)) for spec in scratch],
        compiler_params=pltpu.CompilerParams(vmem_limit_bytes=32 << 20),
        name=name,
    )(*args)


def on_device(psi, potential):
    m, rows, lanes = psi.shape
    orbs = m // 4
    part = (rows, orbs, lanes)
    field = (2, 2 * rows, orbs, lanes)
    face = (2, 4, orbs, lanes)
    matrix = stencil_matrix(lanes // NZ)
    longer = jax.ShapeDtypeStruct((2 * rows + 1, 8, lanes), jnp.float32)
    parts = pl.pallas_call(
        split_kernel,
        out_shape=[longer] * 4,
        in_specs=[pl.BlockSpec(memory_space=pltpu.HBM)] * 2,
        out_specs=[VMEM] * 4,
        scratch_shapes=[
            pltpu.VMEM((4, orbs, rows, lanes), jnp.float32),
            pltpu.VMEM(potential.shape, jnp.float32),
            pltpu.SemaphoreType.DMA((5,)),
        ],
        compiler_params=pltpu.CompilerParams(vmem_limit_bytes=32 << 20),
        name="split",
    )(
        pltpu.with_memory_space_constraint(psi, pltpu.HBM),
        pltpu.with_memory_space_constraint(potential, pltpu.HBM),
    )
    parts = [parts[0]] + [swap(parts[k], Y_MASKS[k]) for k in (1, 2, 3)]
    joined = [field, (2, 2 * rows, 8, lanes), face, face]
    now, v, face1, face2 = call(join_kernel, "join", joined, *parts)
    old = None
    for level in (1, 2, 3):
        left, right = permute(now, y_up), permute(now, y_down)
        face1, face2 = permute(face1, z_even), permute(face2, z_odd)
        args = [now, left, right, face1, face2, v, matrix] + ([] if old is None else [old])
        kernel = functools.partial(level_kernel, level, (0, 1))
        if level < 3:
            outs = call(kernel, f"level{level}", [field, face, face], *args)
            old, (now, face1, face2) = now, outs
        else:
            halves = [
                call(
                    functools.partial(level_kernel, level, (p,)),
                    f"level3_{p}",
                    [part] * 2,
                    *args,
                    scratch=[field[1:]],
                )
                for p in (1, 0)
            ]
            parts = [halves[1][0], halves[0][0], halves[1][1], halves[0][1]]
    parts = [parts[0]] + [swap(parts[k], Y_MASKS[k]) for k in (1, 2, 3)]
    pieces = ((rows, 4 * m, lanes), jnp.bfloat16)
    whole = [(rows, m, lanes)]
    pieces, local = call(gram_kernel, "gram", [pieces, (m, 2 * m)], *parts, scratch=whole)
    ncount = float(rows * lanes * lax.axis_size("gx") * lax.axis_size("gy"))
    kernel = functools.partial(rotate_kernel, ncount)
    return call(kernel, "rotate", [psi.shape], reduce_pairs(local), pieces)


def solution(mesh):
    in_specs = (P(None, "gx", "gy"), P("gx", "gy"))
    out_specs = P(None, "gx", "gy")
    return jax.shard_map(
        on_device, mesh=mesh, in_specs=in_specs, out_specs=out_specs, check_vma=False
    )
```
